256 devices in a mesh: inst: 4 (over y_lo, core), cell: 64 (over z, y_hi, x).
Axes of the slice: x: 4, y: 4 (y_hi: 2, y_lo: 2; y = y_hi * 2 + y_lo), z: 8, core: 2. Of those that a mesh axis runs over, the one named last changes fastest.
Arguments:
- state: float32 [8, 6, 128, 2048], P('inst', None, 'cell'), may hold values from -0.8 to 5, as said below
- pseudo_rate: float32 [128, 2048], P('cell'), may hold values from 0.001 to 0.01
- line_next: int32 [2048], replicated, may hold values from 0 to 2047, each once
- face_codes: int32 [2, 64], replicated, may hold values from 0 to 2
Outputs:
- new_state: float32 [8, 6, 128, 2048], P('inst', None, 'cell')
The draws below stay inside these ranges and needn't reach their ends.
Inputs may be any that keep to these rules, and one draw needn't show every extreme that they name: `state`: conserved variables of a gas with ratio of specific heats 1.4: in every cell density lies between 0.7 and 1.3 and pressure between 0.6 and 1.4. `line_next`: every line is named once. `face_codes`: 0 a slip wall, 1 a fixed inflow state, 2 extrapolation.
All inputs are finite; a program needn't handle non-finite values.
Results may differ from the reference program's by a relative error of at most 0.0003.
Values sent between devices are 32-bit elements; how exact they have to be, the bound alone decides.
A program may use at most 64 MiB of HBM per device.

```python
import math
import jax
import jax.numpy as jnp
import numpy as np
from jax import lax

NT = 8
LINES_DEV = 32
NI = 128
L = 2048
TILES = 64


def draw_state(key, part):
    subkeys = jax.random.split(key, 5)
    grid_shape = (NT, NI, L)
    density = jax.random.uniform(subkeys[0], grid_shape, jnp.float32, 0.7, 1.3)
    pressure = jax.random.uniform(subkeys[1], grid_shape, jnp.float32, 0.6, 1.4)
    axial_speed = 0.5 + jnp.clip(0.3 * jax.random.normal(subkeys[2], grid_shape, jnp.float32), -0.6, 0.6)
    cross_speed = jnp.clip(0.3 * jax.random.normal(subkeys[3], (2,) + grid_shape, jnp.float32), -0.6, 0.6)
    viscous = jnp.exp(jax.random.uniform(subkeys[4], grid_shape, jnp.float32, math.log(0.05), math.log(0.5)))
    kinetic = 0.5 * density * (axial_speed * axial_speed + cross_speed[0] * cross_speed[0] + cross_speed[1] * cross_speed[1])
    energy = pressure / 0.4 + kinetic
    return jnp.stack([density, density * axial_speed, density * cross_speed[0], density * cross_speed[1], energy, density * viscous], axis=1)


def set_ends(entries, own_key, smallest, high):
    longest = entries.shape.index(max(entries.shape))
    spots = []
    for shift in (0, 1):
        where = [jax.random.randint(jax.random.fold_in(own_key, axis), (), 0, length) for axis, length in enumerate(entries.shape)]
        where[longest] = (where[longest] + shift) % entries.shape[longest]
        spots.append(tuple(where))
    return entries.at[spots[0]].set(smallest).at[spots[1]].set(high)


def shard_levels(key, dims, cuts, smallest, largest):
    level = 1.0
    for position, parts in cuts:
        heights = jax.random.uniform(jax.random.fold_in(jax.random.fold_in(key, 6), position), (parts,), jnp.float32, smallest / len(cuts), largest / len(cuts))
        level = level * jnp.repeat(jnp.exp(heights), dims[position] // parts).reshape((-1,) + (1,) * (len(dims) - 1 - position))
    return level


def setup_inputs(seed: int = 0) -> dict:
    key_of = jax.random.split(jax.random.key(seed), 5)
    return {
        "state": draw_state(jax.random.fold_in(key_of[4], 71), 0),
        "pseudo_rate": jnp.clip(jnp.exp(math.log(0.01) - 2.30258502 * jax.random.uniform(key_of[1], (NI, L), jnp.float32) ** shard_levels(key_of[1], (NI, L), ((0, 64),), -0.2, 0.2)), 0.001, 0.01),
        "line_next": jax.random.permutation(key_of[2], L).astype(jnp.int32),
        "face_codes": set_ends(jax.random.randint(key_of[3], (2, TILES), 0, 3), jax.random.fold_in(key_of[3], 1), 0, 2).astype(jnp.int32),
    }


GAMMA_GAS = 1.4
OMEGA_BLADE = 1.0
SENSOR_GAIN = 0.25
FOURTH_GAIN = 0.03125
PITCH_GAIN = 0.5
SECOND_IMPL = 1.0
FOURTH_IMPL = 0.25
FREE_STATE = (1.0, 0.5, 0.0, 0.0, 2.625, 0.2)
MIRROR_SIGNS = (1.0, -1.0, 1.0, 1.0, 1.0, 1.0)
ZERO_BLOCK = (0.0, 0.0, 0.0, 0.0)
UNIT_BLOCK = (1.0, 0.0, 0.0, 1.0)
ZERO_PAIR = (0.0, 0.0)

def spectral_matrix(instances):
    offsets = np.arange(instances)[:, None] - np.arange(instances)[None, :]
    angles = np.pi * offsets / instances
    safe_sin = np.where(offsets == 0, 1.0, np.sin(angles))
    parity = np.where(np.mod(offsets, 2) == 0, -1.0, 1.0)
    matrix_table = np.where(offsets == 0, 0.0, 0.5 * OMEGA_BLADE * parity * np.cos(angles) / safe_sin)
    return jnp.asarray(matrix_table, jnp.float32)

def primitive_parts(cells_state):
    density = cells_state[..., 0, :, :]
    inverse = 1.0 / density
    velocity_x = cells_state[..., 1, :, :] * inverse
    velocity_y = cells_state[..., 2, :, :] * inverse
    velocity_z = cells_state[..., 3, :, :] * inverse
    energy = cells_state[..., 4, :, :]
    pressure = (GAMMA_GAS - 1.0) * (energy - 0.5 * density * (velocity_x * velocity_x + velocity_y * velocity_y + velocity_z * velocity_z))
    sound_speed = jnp.sqrt(GAMMA_GAS * pressure * inverse)
    return (velocity_x, velocity_y, pressure, sound_speed)

def directed_flux(cells_state, normal_velocity, pressure, component):
    zero_plane = jnp.zeros_like(pressure)
    pressure_rows = [zero_plane, zero_plane, zero_plane, zero_plane, pressure * normal_velocity, zero_plane]
    pressure_rows[component] = pressure
    return cells_state * normal_velocity[..., None, :, :] + jnp.stack(pressure_rows, axis=-3)

def line_residual(padded):
    velocity_x, velocity_y, pressure, sound_speed = primitive_parts(padded)
    flux_line = directed_flux(padded, velocity_x, pressure, 1)
    radius = jnp.abs(velocity_x) + sound_speed
    sensor = jnp.abs(pressure[..., 2:, :] - 2.0 * pressure[..., 1:-1, :] + pressure[..., :-2, :]) / (pressure[..., 2:, :] + 2.0 * pressure[..., 1:-1, :] + pressure[..., :-2, :])
    second = SENSOR_GAIN * jnp.maximum(sensor[..., :-1, :], sensor[..., 1:, :])
    fourth = jnp.maximum(0.0, FOURTH_GAIN - second)
    face_radius = 0.5 * (radius[..., 1:-2, :] + radius[..., 2:-1, :])
    left_far = padded[..., :-3, :]
    left_near = padded[..., 1:-2, :]
    right_near = padded[..., 2:-1, :]
    right_far = padded[..., 3:, :]
    damping = face_radius[..., None, :, :] * (second[..., None, :, :] * (right_near - left_near) - fourth[..., None, :, :] * (right_far - 3.0 * right_near + 3.0 * left_near - left_far))
    face_flux = 0.5 * (flux_line[..., 1:-2, :] + flux_line[..., 2:-1, :]) - damping
    return (face_flux[..., 1:, :] - face_flux[..., :-1, :], radius)

def pitch_residual(cells_state, next_lines, prev_lines):
    velocity_x, velocity_y, pressure, sound_speed = primitive_parts(cells_state)
    pitch_flux = directed_flux(cells_state, velocity_y, pressure, 2)
    radius = jnp.abs(velocity_y) + sound_speed
    state_next = jnp.take(cells_state, next_lines, axis=-1)
    flux_next = jnp.take(pitch_flux, next_lines, axis=-1)
    radius_next = jnp.take(radius, next_lines, axis=-1)
    face_flux = 0.5 * (pitch_flux + flux_next) - PITCH_GAIN * (0.5 * (radius + radius_next))[..., None, :, :] * (state_next - cells_state)
    return face_flux - jnp.take(face_flux, prev_lines, axis=-1)

def boundary_cells(edge_pair, line_codes, lower_end):
    reflected = edge_pair[..., ::-1, :] * jnp.asarray(MIRROR_SIGNS, jnp.float32)[:, None, None]
    if lower_end:
        copied = jnp.concatenate([edge_pair[..., :1, :], edge_pair[..., :1, :]], axis=-2)
    else:
        copied = jnp.concatenate([edge_pair[..., 1:, :], edge_pair[..., 1:, :]], axis=-2)
    inflow = jnp.asarray(FREE_STATE, jnp.float32)[:, None, None] + jnp.zeros_like(edge_pair)
    return jnp.where(line_codes == 0, reflected, jnp.where(line_codes == 1, inflow, copied))

def line_coefficients(radius_ext, diagonal_term, positions, total_cells):
    radius_below = radius_ext[..., :-2, :]
    radius_centre = radius_ext[..., 1:-1, :]
    radius_above = radius_ext[..., 2:, :]
    face_below = 0.5 * (radius_below + radius_centre)
    face_above = 0.5 * (radius_centre + radius_above)
    far_low = FOURTH_IMPL * radius_below
    near_low = -SECOND_IMPL * face_below - 2.0 * FOURTH_IMPL * (radius_below + radius_centre)
    middle = diagonal_term + SECOND_IMPL * (face_below + face_above) + FOURTH_IMPL * (radius_below + 4.0 * radius_centre + radius_above)
    near_high = -SECOND_IMPL * face_above - 2.0 * FOURTH_IMPL * (radius_centre + radius_above)
    far_high = FOURTH_IMPL * radius_above
    column = positions[:, None]
    far_low = jnp.where(column >= 2, far_low, 0.0)
    near_low = jnp.where(column >= 1, near_low, 0.0)
    near_high = jnp.where(column <= total_cells - 2, near_high, 0.0)
    far_high = jnp.where(column <= total_cells - 3, far_high, 0.0)
    return (far_low, near_low, middle, near_high, far_high)

def block_product(first_matrix, second_matrix):
    return (first_matrix[0] * second_matrix[0] + first_matrix[1] * second_matrix[2], first_matrix[0] * second_matrix[1] + first_matrix[1] * second_matrix[3], first_matrix[2] * second_matrix[0] + first_matrix[3] * second_matrix[2], first_matrix[2] * second_matrix[1] + first_matrix[3] * second_matrix[3])

def block_inverse(matrix):
    determinant = matrix[0] * matrix[3] - matrix[1] * matrix[2]
    reciprocal = 1.0 / determinant
    return (matrix[3] * reciprocal, -matrix[1] * reciprocal, -matrix[2] * reciprocal, matrix[0] * reciprocal)

def block_apply(matrix, vector):
    return (matrix[0] * vector[0] + matrix[1] * vector[1], matrix[2] * vector[0] + matrix[3] * vector[1])

def add_blocks(first_members, second_members):
    return tuple((a + b for a, b in zip(first_members, second_members)))

def negate(members):
    return tuple((-a for a in members))

def extend_blocks(members, fill_values):
    return tuple((jnp.concatenate([m, jnp.full_like(m[..., :1, :], f)], axis=-2) for m, f in zip(members, fill_values)))

def shift_next(members, fill_values):
    return tuple((jnp.concatenate([m[..., 1:, :], jnp.full_like(m[..., :1, :], f)], axis=-2) for m, f in zip(members, fill_values)))

def shift_prev(members):
    return tuple((jnp.concatenate([jnp.zeros_like(m[..., :1, :]), m[..., :-1, :]], axis=-2) for m in members))

def pair_split(member):
    shaped = member.reshape(member.shape[:-2] + (member.shape[-2] // 2, 2, member.shape[-1]))
    return (shaped[..., 0, :], shaped[..., 1, :])

def split_parity(members):
    halves = [pair_split(m) for m in members]
    return (tuple((h[0] for h in halves)), tuple((h[1] for h in halves)))

def alternate(first_member, second_member):
    stacked = jnp.stack((first_member, second_member), axis=-2)
    return stacked.reshape(first_member.shape[:-2] + (2 * first_member.shape[-2], first_member.shape[-1]))

def reduce_blocks(sub_blocks, diag_blocks, super_blocks, right_side):
    block_count = diag_blocks[0].shape[-2]
    if block_count == 1:
        return block_apply(block_inverse(diag_blocks), right_side)
    if block_count % 2 == 1:
        sub_blocks = extend_blocks(sub_blocks, ZERO_BLOCK)
        diag_blocks = extend_blocks(diag_blocks, UNIT_BLOCK)
        super_blocks = extend_blocks(super_blocks, ZERO_BLOCK)
        right_side = extend_blocks(right_side, ZERO_PAIR)
    sub_even, sub_odd = split_parity(sub_blocks)
    diag_even, diag_odd = split_parity(diag_blocks)
    super_even, super_odd = split_parity(super_blocks)
    side_even, side_odd = split_parity(right_side)
    inverse_even = block_inverse(diag_even)
    inverse_next = shift_next(inverse_even, UNIT_BLOCK)
    sub_next = shift_next(sub_even, ZERO_BLOCK)
    super_next = shift_next(super_even, ZERO_BLOCK)
    side_next = shift_next(side_even, ZERO_PAIR)
    left_factor = negate(block_product(sub_odd, inverse_even))
    right_factor = negate(block_product(super_odd, inverse_next))
    reduced_sub = block_product(left_factor, sub_even)
    reduced_diag = add_blocks(diag_odd, add_blocks(block_product(left_factor, super_even), block_product(right_factor, sub_next)))
    reduced_super = block_product(right_factor, super_next)
    reduced_side = add_blocks(side_odd, add_blocks(block_apply(left_factor, side_even), block_apply(right_factor, side_next)))
    odd_values = reduce_blocks(reduced_sub, reduced_diag, reduced_super, reduced_side)
    before_values = shift_prev(odd_values)
    remainder = add_blocks(side_even, negate(add_blocks(block_apply(sub_even, before_values), block_apply(super_even, odd_values))))
    even_values = block_apply(inverse_even, remainder)
    merged = tuple((alternate(e, o) for e, o in zip(even_values, odd_values)))
    return tuple((m[..., :block_count, :] for m in merged))

def line_solve(coefficients, right_side):
    pairs_list = [pair_split(m[:, None]) for m in coefficients]
    zero_plane = jnp.zeros_like(pairs_list[2][0])
    sub_blocks = (pairs_list[0][0], pairs_list[1][0], zero_plane, pairs_list[0][1])
    diag_blocks = (pairs_list[2][0], pairs_list[3][0], pairs_list[1][1], pairs_list[2][1])
    super_blocks = (pairs_list[4][0], zero_plane, pairs_list[3][1], pairs_list[4][1])
    values = reduce_blocks(sub_blocks, diag_blocks, super_blocks, pair_split(right_side))
    return alternate(values[0], values[1])

def reference(state, pseudo_rate, line_next, face_codes):
    spectral = spectral_matrix(NT)
    source_time = jnp.einsum('nm,mvil->nvil', spectral, state, precision=lax.Precision.HIGHEST)
    prev_lines = jnp.zeros_like(line_next).at[line_next].set(jnp.arange(L, dtype=jnp.int32))
    codes_lines = jnp.repeat(face_codes, LINES_DEV, axis=1)

    def one_instance(inputs):
        cells_state, time_term = inputs
        lower_ghost = boundary_cells(cells_state[:, 0:2, :], codes_lines[0], True)
        upper_ghost = boundary_cells(cells_state[:, -2:, :], codes_lines[1], False)
        padded = jnp.concatenate([lower_ghost, cells_state, upper_ghost], axis=1)
        line_part, radius = line_residual(padded)
        residual = line_part + pitch_residual(cells_state, line_next, prev_lines) + time_term
        centre_radius = radius[2:-2, :]
        radius_ext = jnp.pad(centre_radius, ((1, 1), (0, 0)))
        coefficients = line_coefficients(radius_ext, pseudo_rate * centre_radius, jnp.arange(NI, dtype=jnp.int32), NI)
        update = line_solve(tuple((c[None] for c in coefficients)), -residual[None])
        return cells_state + update[0]
    return lax.map(one_instance, (state, source_time))
```

```python
import jax
import jax.numpy as jnp
import numpy as np
from jax import lax
from jax.experimental import pallas as pl
from jax.experimental.pallas import tpu as pltpu
from jax.sharding import PartitionSpec as P

NT = 8
CELLS = 64
CHUNKS = 16
LANES = 128
TILE_LINES = 32
GAMMA_GAS = 1.4
FREE_STATE = (1.0, 0.5, 0.0, 0.0, 2.625, 0.2)
F32 = jnp.float32
FACTOR_PLANES = 168


def spectral_table():
    offsets = np.arange(NT)[:, None] - np.arange(NT)[None, :]
    angles = np.pi * offsets / NT
    safe_sin = np.where(offsets == 0, 1.0, np.sin(angles))
    parity = np.where(np.mod(offsets, 2) == 0, -1.0, 1.0)
    return np.where(offsets == 0, 0.0, 0.5 * parity * np.cos(angles) / safe_sin)


def time_weight(inst, row, slot, column):
    table = spectral_table()
    values = [float(table[2 * i + row, 2 * (i ^ slot) + column]) for i in range(NT // 2)]
    weight = jnp.float32(values[3])
    for i in (2, 1, 0):
        weight = jnp.where(inst == i, jnp.float32(values[i]), weight)
    return weight


def primitives(cell):
    inverse = 1.0 / cell[0]
    vel_x = cell[1] * inverse
    vel_y = cell[2] * inverse
    vel_z = cell[3] * inverse
    pressure = 0.4 * (cell[4] - 0.5 * cell[0] * (vel_x * vel_x + vel_y * vel_y + vel_z * vel_z))
    sound = jnp.sqrt(GAMMA_GAS * pressure * inverse)
    return vel_x, vel_y, pressure, sound


def flux(cell, velocity, pressure, component):
    rows = [cell[v] * velocity for v in range(6)]
    rows[component] = rows[component] + pressure
    rows[4] = rows[4] + pressure * velocity
    return rows


def line_part(cells):
    parts = [primitives(c) for c in cells]
    pressure = [q[2] for q in parts]
    radius = [jnp.abs(q[0]) + q[3] for q in parts]
    fluxes = [flux(cells[j], parts[j][0], pressure[j], 1) for j in range(1, 5)]
    sensor = [
        jnp.abs(pressure[j + 1] - 2.0 * pressure[j] + pressure[j - 1])
        / (pressure[j + 1] + 2.0 * pressure[j] + pressure[j - 1])
        for j in range(1, 5)
    ]
    faces = []
    for j in range(1, 4):
        second = 0.25 * jnp.maximum(sensor[j - 1], sensor[j])
        fourth = jnp.maximum(0.0, 0.03125 - second)
        face_radius = 0.5 * (radius[j] + radius[j + 1])
        rows = []
        for v in range(6):
            near = cells[j + 1][v] - cells[j][v]
            far = cells[j + 2][v] - cells[j - 1][v] - 3.0 * near
            rows.append(
                0.5 * (fluxes[j - 1][v] + fluxes[j][v])
                - face_radius * (second * near - fourth * far)
            )
        faces.append(rows)
    return [[faces[c + 1][v] - faces[c][v] for v in range(6)] for c in range(2)]


def ghost_cells(near, far, codes):
    inflow = [jnp.full(codes.shape, FREE_STATE[v], F32) for v in range(6)]

    def pick(mirror, v):
        reflected = -mirror[v] if v == 1 else mirror[v]
        return jnp.where(codes == 0, reflected, jnp.where(codes == 1, inflow[v], near[v]))

    return [pick(near, v) for v in range(6)], [pick(far, v) for v in range(6)]


def mat_mat(a, b):
    return (
        a[0] * b[0] + a[1] * b[2],
        a[0] * b[1] + a[1] * b[3],
        a[2] * b[0] + a[3] * b[2],
        a[2] * b[1] + a[3] * b[3],
    )


def mat_vec(a, x):
    return (a[0] * x[0] + a[1] * x[1], a[2] * x[0] + a[3] * x[1])


def mat_inv(m):
    reciprocal = 1.0 / (m[0] * m[3] - m[1] * m[2])
    return (m[3] * reciprocal, -m[1] * reciprocal, -m[2] * reciprocal, m[0] * reciprocal)


def plus(a, b):
    return tuple(x + y for x, y in zip(a, b))


def minus(a):
    return tuple(-x for x in a)


def rolled(members, shift, axis):
    return tuple(pltpu.roll(m, shift % 8, axis) for m in members)


STEPS = (
    (0, 1, 2, False),
    (2, 3, 4, False),
    (4, 5, 6, False),
    (6, 7, 0, True),
    (1, 3, 5, False),
    (5, 7, 1, True),
    (3, 7, 3, True),
)
BEFORE = {0: (7, True), 2: (1, False), 4: (3, False), 6: (5, False), 1: (7, True), 5: (3, False), 3: (7, True)}
AFTER = {0: 1, 2: 3, 4: 5, 6: 7, 1: 3, 5: 7, 3: 7}


def factorise(coef_ref, fac_ref):
    def rows(kind, v):
        return coef_ref[kind, 8 * v : 8 * v + 8, :]

    plane = lax.broadcasted_iota(jnp.int32, (8, LANES), 0)
    low = [rows(0, v) for v in range(8)]
    high = [rows(1, v) for v in range(8)]
    before = [jnp.where(plane == 0, 0.0, pltpu.roll(high[7], 1, 0))] + high[:7]
    after = low[1:] + [jnp.where(plane == 7, 0.0, pltpu.roll(low[0], 7, 0))]
    zero = jnp.zeros((8, LANES), F32)
    sub, diag, sup = {}, {}, {}
    for v in range(8):
        a, b, c, d = before[v], low[v], high[v], after[v]
        mid_low = rows(2, v) * b + 0.5 * (a + 2.0 * b + c) + 0.25 * (a + 4.0 * b + c)
        mid_high = rows(3, v) * c + 0.5 * (b + 2.0 * c + d) + 0.25 * (b + 4.0 * c + d)
        sub[v] = (0.25 * a, -(a + b), zero, 0.25 * b)
        diag[v] = (mid_low, -(b + c), -(b + c), mid_high)
        sup[v] = (0.25 * c, zero, -(c + d), 0.25 * d)
    sub[0] = tuple(jnp.where(plane == 0, 0.0, m) for m in sub[0])
    sup[7] = tuple(jnp.where(plane == 7, 0.0, m) for m in sup[7])
    count = [0]

    def keep(members):
        for m in members:
            fac_ref[count[0]] = m
            count[0] += 1

    inverse = {}
    for e, o, n, wraps in STEPS:
        for x in (e, n):
            if x not in inverse:
                inverse[x] = mat_inv(diag[x])
        inv_n, sub_n, sup_n = inverse[n], sub[n], sup[n]
        if wraps:
            inv_n, sub_n, sup_n = rolled(inv_n, -1, 0), rolled(sub_n, -1, 0), rolled(sup_n, -1, 0)
        left = minus(mat_mat(sub[o], inverse[e]))
        right = minus(mat_mat(sup[o], inv_n))
        keep(left)
        keep(right)
        keep(inverse[e])
        keep(mat_mat(inverse[e], sub[e]))
        keep(mat_mat(inverse[e], sup[e]))
        sub[o] = mat_mat(left, sub[e])
        diag[o] = plus(diag[o], plus(mat_mat(left, sup[e]), mat_mat(right, sub_n)))
        sup[o] = mat_mat(right, sup_n)
    s, d, u = sub[7], diag[7], sup[7]
    for h in (1, 2, 4):
        inv = mat_inv(d)
        left = minus(mat_mat(s, rolled(inv, h, 0)))
        right = minus(mat_mat(u, rolled(inv, -h, 0)))
        keep(left)
        keep(right)
        s_low, u_low = rolled(s, h, 0), rolled(u, h, 0)
        s_high, u_high = rolled(s, -h, 0), rolled(u, -h, 0)
        d = plus(d, plus(mat_mat(left, u_low), mat_mat(right, s_high)))
        s, u = mat_mat(left, s_low), mat_mat(right, u_high)
    keep(mat_inv(d))


def substitute(fac_ref, side_ref, out_ref):
    def fac(first):
        return tuple(fac_ref[first + j][None] for j in range(4))

    r = [
        tuple(side_ref[:, c, 8 * v : 8 * v + 8, :] for c in range(2)) for v in range(8)
    ]
    at = 0
    bases = {}
    for e, o, n, wraps in STEPS:
        side_n = rolled(r[n], -1, 1) if wraps else r[n]
        r[o] = plus(r[o], plus(mat_vec(fac(at), r[e]), mat_vec(fac(at + 4), side_n)))
        bases[e] = at + 8
        at += 20
    x = r[7]
    for h in (1, 2, 4):
        x = plus(
            x,
            plus(mat_vec(fac(at), rolled(x, h, 1)), mat_vec(fac(at + 4), rolled(x, -h, 1))),
        )
        at += 8
    values = {7: mat_vec(fac(at), x)}
    for e in (3, 5, 1, 6, 4, 2, 0):
        base = bases[e]
        prior, wraps = BEFORE[e]
        low = rolled(values[prior], 1, 1) if wraps else values[prior]
        back = plus(mat_vec(fac(base + 4), low), mat_vec(fac(base + 8), values[AFTER[e]]))
        values[e] = tuple(a - b for a, b in zip(mat_vec(fac(base), r[e]), back))
    for v in range(8):
        for c in range(2):
            out_ref[:, c, 8 * v : 8 * v + 8, :] = values[v][c]


def invert_lines(next_ref, prev_ref):
    lane = lax.broadcasted_iota(jnp.int32, (CHUNKS, LANES), 1).astype(F32)
    chunk = lax.broadcasted_iota(jnp.int32, (CHUNKS, LANES), 0)
    slot = lax.broadcasted_iota(jnp.int32, (LANES, LANES), 0)

    def body(q, total):
        row = next_ref[pl.ds(q, 1), :]
        hit = jnp.broadcast_to(row >> 7, (CHUNKS, LANES)) == chunk
        place = jnp.where(jnp.broadcast_to(row & 127, (LANES, LANES)) == slot, 1.0, 0.0)
        left = jnp.concatenate([jnp.where(hit, lane, 0.0), jnp.where(hit, 1.0, 0.0)], axis=0)
        found = lax.dot_general(
            left.astype(jnp.bfloat16),
            place.astype(jnp.bfloat16),
            (((1,), (1,)), ((), ())),
            preferred_element_type=F32,
        )
        return total + found[:CHUNKS] + found[CHUNKS:] * (q.astype(F32) * 128.0)

    total = lax.fori_loop(0, CHUNKS, body, jnp.zeros((CHUNKS, LANES), F32))
    prev_ref[...] = total.astype(jnp.int32)


def gather_lines(source, target, index_ref):
    source_rows = source.reshape(24 * CHUNKS, LANES)
    target_rows = target.reshape(24 * CHUNKS, LANES)

    def body(c, carry):
        row = jnp.broadcast_to(index_ref[pl.ds(c, 1), :], (8, LANES))
        lane = row & 127
        chunk = row >> 7
        found = [jnp.zeros((8, LANES), F32) for _ in range(3)]
        for s in range(CHUNKS):
            hit = chunk == s
            for g in range(3):
                rows = source_rows[pl.ds(g * 8 * CHUNKS + s, 8, stride=CHUNKS), :]
                found[g] = jnp.where(hit, jnp.take_along_axis(rows, lane, axis=1), found[g])
        for g in range(3):
            target_rows[pl.ds(g * 8 * CHUNKS + c, 8, stride=CHUNKS), :] = found[g]
        return carry

    lax.fori_loop(0, CHUNKS, body, 0)


def kernel(
    state_ref, rate_ref, next_ref, codes_ref, out_ref,
    own, low, high, other, shifted, kflux, kprev, rhs, lp, prev, codes, coef, fac, side, delta,
    load_sem, ghost_sem, inst_sem, coef_sem, side_sem, back_sem, self_sem,
):
    me = lax.axis_index("cell")
    inst = lax.axis_index("inst")
    barrier = pltpu.get_barrier_semaphore()

    def greet(j, carry):
        pl.semaphore_signal(barrier, 1, device_id={"cell": lax.rem(me + j, CELLS)})
        return carry

    lax.fori_loop(1, CELLS, greet, 0)
    for j in range(1, 4):
        pl.semaphore_signal(barrier, 1, device_id={"inst": inst ^ j})

    loads = [
        pltpu.make_async_copy(state_ref.at[:, :, :, c], own.at[:, :, c], load_sem.at[c])
        for c in range(2)
    ] + [
        pltpu.make_async_copy(rate_ref.at[:, c], lp.at[i, 2 + c], load_sem.at[2 + 2 * i + c])
        for i in range(2)
        for c in range(2)
    ]
    for copy in loads:
        copy.start()
    invert_lines(next_ref, prev)
    codes[...] = jnp.zeros((8, LANES), jnp.int32)
    codes[0:2, 0:64] = codes_ref[...]
    for copy in loads:
        copy.wait()

    def own_radius(i, carry):
        for c in range(2):
            vel_x, _, _, sound = primitives([own[i, v, c] for v in range(6)])
            lp[i, c] = jnp.abs(vel_x) + sound
        return carry

    lax.fori_loop(0, 2, own_radius, 0)
    gather_lines(own, shifted, next_ref)

    pl.semaphore_wait(barrier, CELLS - 1 + 3)

    right = lax.rem(me + 1, CELLS)
    left = lax.rem(me + CELLS - 1, CELLS)
    to_pair = pltpu.make_async_remote_copy(
        own, other.at[1], inst_sem.at[0], inst_sem.at[1], device_id={"inst": inst ^ 2}
    )
    to_pair.start()
    to_right = pltpu.make_async_remote_copy(
        own, low, ghost_sem.at[0], ghost_sem.at[1], device_id={"cell": right}
    )
    to_right.start()
    to_left = pltpu.make_async_remote_copy(
        own, high, ghost_sem.at[2], ghost_sem.at[3], device_id={"cell": left}
    )
    to_left.start()
    to_twin = pltpu.make_async_remote_copy(
        own, other.at[0], inst_sem.at[2], inst_sem.at[3], device_id={"inst": inst ^ 1}
    )
    to_twin.start()

    my_row = (me & 7) * 8 + (me >> 3)

    def send_coef(j, carry):
        peer = lax.rem(me + j, CELLS)
        pltpu.make_async_remote_copy(
            lp.at[peer >> 5, :, peer & 15],
            coef.at[:, my_row],
            coef_sem.at[0],
            coef_sem.at[1],
            device_id={"cell": peer},
        ).start()
        return carry

    lax.fori_loop(1, CELLS, send_coef, 0)
    my_coef = pltpu.make_async_copy(lp.at[me >> 5, :, me & 15], coef.at[:, my_row], self_sem.at[0])
    my_coef.start()

    def pitch_flux(i, carry):
        for c in range(2):
            here = [own[i, v, c] for v in range(6)]
            there = [shifted[i, v, c] for v in range(6)]
            _, vel_h, p_h, sound_h = primitives(here)
            _, vel_t, p_t, sound_t = primitives(there)
            flux_h = flux(here, vel_h, p_h, 2)
            flux_t = flux(there, vel_t, p_t, 2)
            radius = 0.25 * (jnp.abs(vel_h) + sound_h + jnp.abs(vel_t) + sound_t)
            for v in range(6):
                kflux[i, v, c] = 0.5 * (flux_h[v] + flux_t[v]) - radius * (there[v] - here[v])
        return carry

    lax.fori_loop(0, 2, pitch_flux, 0)
    gather_lines(kflux, kprev, prev)

    to_pair.wait_recv()
    to_forward = pltpu.make_async_remote_copy(
        other.at[1], other.at[2], inst_sem.at[4], inst_sem.at[5], device_id={"inst": inst ^ 1}
    )
    to_forward.start()

    pltpu.make_async_copy(
        coef.at[:, pl.ds(0, CELLS - 1)], coef.at[:, pl.ds(0, CELLS - 1)], coef_sem.at[1]
    ).wait()
    my_coef.wait()
    factorise(coef, fac)

    to_right.wait_recv()
    to_left.wait_recv()
    spread = lax.broadcasted_iota(jnp.int32, (CHUNKS, LANES), 0) * 4 + (
        lax.broadcasted_iota(jnp.int32, (CHUNKS, LANES), 1) // TILE_LINES
    )
    end_codes = [
        jnp.take_along_axis(jnp.broadcast_to(codes[e : e + 1, :], (CHUNKS, LANES)), spread, axis=1)
        for e in range(2)
    ]
    first = me == 0
    last = me == CELLS - 1

    def add_line(i, carry):
        mine = [[own[i, v, c] for v in range(6)] for c in range(2)]
        low_near, low_far = ghost_cells(mine[0], mine[1], end_codes[0])
        high_near, high_far = ghost_cells(mine[1], mine[0], end_codes[1])
        cells = [
            [jnp.where(first, low_far[v], low[i, v, 0]) for v in range(6)],
            [jnp.where(first, low_near[v], low[i, v, 1]) for v in range(6)],
            mine[0],
            mine[1],
            [jnp.where(last, high_near[v], high[i, v, 0]) for v in range(6)],
            [jnp.where(last, high_far[v], high[i, v, 1]) for v in range(6)],
        ]
        parts = line_part(cells)
        for c in range(2):
            for v in range(6):
                rhs[i, v, c] = kprev[i, v, c] - kflux[i, v, c] - parts[c][v]
        return carry

    lax.fori_loop(0, 2, add_line, 0)
    to_twin.wait_recv()
    to_forward.wait_recv()
    weights = [
        [[time_weight(inst, n, slot, m) for m in range(2)] for slot in range(4)] for n in range(2)
    ]

    def add_time(v, carry):
        for c in range(2):
            planes = [[own[m, v, c] for m in range(2)]] + [
                [other[slot, m, v, c] for m in range(2)] for slot in range(3)
            ]
            for n in range(2):
                total = rhs[n, v, c]
                for slot in range(4):
                    for m in range(2):
                        if slot == 0 and m == n:
                            continue
                        total = total - weights[n][slot][m] * planes[slot][m]
                rhs[n, v, c] = total
        return carry

    lax.fori_loop(0, 6, add_time, 0)

    def send_side(j, carry):
        peer = lax.rem(me + j, CELLS)
        pltpu.make_async_remote_copy(
            rhs.at[peer >> 5, pl.ds(((peer >> 4) & 1) * 3, 3), :, peer & 15],
            side.at[:, :, my_row],
            side_sem.at[0],
            side_sem.at[1],
            device_id={"cell": peer},
        ).start()
        return carry

    lax.fori_loop(1, CELLS, send_side, 0)
    my_inst, my_var, my_chunk = me >> 5, ((me >> 4) & 1) * 3, me & 15
    my_side = pltpu.make_async_copy(
        rhs.at[my_inst, pl.ds(my_var, 3), :, my_chunk], side.at[:, :, my_row], self_sem.at[1]
    )
    my_side.start()
    many = side.at[:, :, pl.ds(0, CELLS - 1)]
    pltpu.make_async_copy(many, many, side_sem.at[1]).wait()
    my_side.wait()
    substitute(fac, side, delta)

    def send_back(j, carry):
        peer = lax.rem(me + j, CELLS)
        pltpu.make_async_remote_copy(
            delta.at[:, :, (peer & 7) * 8 + (peer >> 3)],
            out_ref.at[my_inst, pl.ds(my_var, 3), my_chunk],
            back_sem.at[0],
            back_sem.at[1],
            device_id={"cell": peer},
        ).start()
        return carry

    lax.fori_loop(1, CELLS, send_back, 0)
    my_back = pltpu.make_async_copy(
        delta.at[:, :, my_row], out_ref.at[my_inst, pl.ds(my_var, 3), my_chunk], self_sem.at[2]
    )
    my_back.start()
    for copy in (to_pair, to_right, to_left, to_twin, to_forward):
        copy.wait_send()
    few = coef.at[:, pl.ds(0, CELLS - 1)]
    pltpu.make_async_copy(few, few, coef_sem.at[0]).wait()
    pltpu.make_async_copy(many, many, side_sem.at[0]).wait()
    pltpu.make_async_copy(many, many, back_sem.at[0]).wait()
    pltpu.make_async_copy(many, many, back_sem.at[1]).wait()
    my_back.wait()


def local(state, pseudo_rate, line_next, face_codes):
    view = state.reshape(2, 6, 2, CHUNKS, LANES).transpose(0, 1, 3, 2, 4)
    rate = pseudo_rate.reshape(2, CHUNKS, LANES).transpose(1, 0, 2)
    block = (2, 6, 2, CHUNKS, LANES)
    in_vmem = pl.BlockSpec(memory_space=pltpu.VMEM)
    in_place = pl.BlockSpec(memory_space=pl.ANY)
    dma = pltpu.SemaphoreType.DMA
    update = pl.pallas_call(
        kernel,
        out_shape=jax.ShapeDtypeStruct((2, 6, CHUNKS, 2, LANES), F32),
        in_specs=[in_place, in_place, in_vmem, in_vmem],
        out_specs=in_vmem,
        scratch_shapes=[
            pltpu.VMEM(block, F32),
            pltpu.VMEM(block, F32),
            pltpu.VMEM(block, F32),
            pltpu.VMEM((3,) + block, F32),
            pltpu.VMEM(block, F32),
            pltpu.VMEM(block, F32),
            pltpu.VMEM(block, F32),
            pltpu.VMEM(block, F32),
            pltpu.VMEM((2, 4, CHUNKS, LANES), F32),
            pltpu.VMEM((CHUNKS, LANES), jnp.int32),
            pltpu.VMEM((8, LANES), jnp.int32),
            pltpu.VMEM((4, CELLS, LANES), F32),
            pltpu.VMEM((FACTOR_PLANES, 8, LANES), F32),
            pltpu.VMEM((3, 2, CELLS, LANES), F32),
            pltpu.VMEM((3, 2, CELLS, LANES), F32),
            dma((6,)),
            dma((4,)),
            dma((6,)),
            dma((2,)),
            dma((2,)),
            dma((2,)),
            dma((3,)),
        ],
        compiler_params=pltpu.CompilerParams(collective_id=0, has_side_effects=True),
        name="line_implicit_step",
    )(view, rate, line_next.reshape(CHUNKS, LANES), face_codes)
    return state + update.transpose(0, 1, 3, 2, 4).reshape(state.shape)


def solution(mesh):
    placed = (P("inst", None, "cell", None), P("cell", None), P(), P())
    return jax.shard_map(
        local, mesh=mesh, in_specs=placed, out_specs=P("inst", None, "cell", None), check_vma=False
    )
```

```python
import jax
import jax.numpy as jnp
import numpy as np
from jax import lax
from jax.experimental import pallas as pl
from jax.experimental.pallas import tpu as pltpu
from jax.sharding import PartitionSpec as P

NT = 8
CELLS = 64
CHUNKS = 16
LANES = 128
TILE_LINES = 32
GAMMA_GAS = 1.4
FREE_STATE = (1.0, 0.5, 0.0, 0.0, 2.625, 0.2)
F32 = jnp.float32
FACTOR_PLANES = 168


def spectral_table():
    offsets = np.arange(NT)[:, None] - np.arange(NT)[None, :]
    angles = np.pi * offsets / NT
    safe_sin = np.where(offsets == 0, 1.0, np.sin(angles))
    parity = np.where(np.mod(offsets, 2) == 0, -1.0, 1.0)
    return np.where(offsets == 0, 0.0, 0.5 * parity * np.cos(angles) / safe_sin)


def time_weight(inst, row, slot, column):
    table = spectral_table()
    values = [float(table[2 * i + row, 2 * (i ^ slot) + column]) for i in range(NT // 2)]
    weight = jnp.float32(values[3])
    for i in (2, 1, 0):
        weight = jnp.where(inst == i, jnp.float32(values[i]), weight)
    return weight


def primitives(cell):
    inverse = 1.0 / cell[0]
    vel_x = cell[1] * inverse
    vel_y = cell[2] * inverse
    vel_z = cell[3] * inverse
    pressure = 0.4 * (cell[4] - 0.5 * cell[0] * (vel_x * vel_x + vel_y * vel_y + vel_z * vel_z))
    sound = jnp.sqrt(GAMMA_GAS * pressure * inverse)
    return vel_x, vel_y, pressure, sound


def flux(cell, velocity, pressure, component):
    rows = [cell[v] * velocity for v in range(6)]
    rows[component] = rows[component] + pressure
    rows[4] = rows[4] + pressure * velocity
    return rows


def line_part(cells):
    parts = [primitives(c) for c in cells]
    pressure = [q[2] for q in parts]
    radius = [jnp.abs(q[0]) + q[3] for q in parts]
    fluxes = [flux(cells[j], parts[j][0], pressure[j], 1) for j in range(1, 5)]
    sensor = [
        jnp.abs(pressure[j + 1] - 2.0 * pressure[j] + pressure[j - 1])
        / (pressure[j + 1] + 2.0 * pressure[j] + pressure[j - 1])
        for j in range(1, 5)
    ]
    faces = []
    for j in range(1, 4):
        second = 0.25 * jnp.maximum(sensor[j - 1], sensor[j])
        fourth = jnp.maximum(0.0, 0.03125 - second)
        face_radius = 0.5 * (radius[j] + radius[j + 1])
        rows = []
        for v in range(6):
            near = cells[j + 1][v] - cells[j][v]
            far = cells[j + 2][v] - cells[j - 1][v] - 3.0 * near
            rows.append(
                0.5 * (fluxes[j - 1][v] + fluxes[j][v])
                - face_radius * (second * near - fourth * far)
            )
        faces.append(rows)
    return [[faces[c + 1][v] - faces[c][v] for v in range(6)] for c in range(2)]


def ghost_cells(near, far, codes):
    inflow = [jnp.full(codes.shape, FREE_STATE[v], F32) for v in range(6)]

    def pick(mirror, v):
        reflected = -mirror[v] if v == 1 else mirror[v]
        return jnp.where(codes == 0, reflected, jnp.where(codes == 1, inflow[v], near[v]))

    return [pick(near, v) for v in range(6)], [pick(far, v) for v in range(6)]


def mat_mat(a, b):
    return (
        a[0] * b[0] + a[1] * b[2],
        a[0] * b[1] + a[1] * b[3],
        a[2] * b[0] + a[3] * b[2],
        a[2] * b[1] + a[3] * b[3],
    )


def mat_vec(a, x):
    return (a[0] * x[0] + a[1] * x[1], a[2] * x[0] + a[3] * x[1])


def mat_inv(m):
    reciprocal = 1.0 / (m[0] * m[3] - m[1] * m[2])
    return (m[3] * reciprocal, -m[1] * reciprocal, -m[2] * reciprocal, m[0] * reciprocal)


def plus(a, b):
    return tuple(x + y for x, y in zip(a, b))


def minus(a):
    return tuple(-x for x in a)


def rolled(members, shift, axis):
    return tuple(pltpu.roll(m, shift % 8, axis) for m in members)


STEPS = (
    (0, 1, 2, False),
    (2, 3, 4, False),
    (4, 5, 6, False),
    (6, 7, 0, True),
    (1, 3, 5, False),
    (5, 7, 1, True),
    (3, 7, 3, True),
)
BEFORE = {0: (7, True), 2: (1, False), 4: (3, False), 6: (5, False), 1: (7, True), 5: (3, False), 3: (7, True)}
AFTER = {0: 1, 2: 3, 4: 5, 6: 7, 1: 3, 5: 7, 3: 7}


def factorise(coef_ref, fac_ref):
    def rows(kind, v):
        return coef_ref[kind, 8 * v : 8 * v + 8, :]

    plane = lax.broadcasted_iota(jnp.int32, (8, LANES), 0)
    low = [rows(0, v) for v in range(8)]
    high = [rows(1, v) for v in range(8)]
    before = [jnp.where(plane == 0, 0.0, pltpu.roll(high[7], 1, 0))] + high[:7]
    after = low[1:] + [jnp.where(plane == 7, 0.0, pltpu.roll(low[0], 7, 0))]
    zero = jnp.zeros((8, LANES), F32)
    sub, diag, sup = {}, {}, {}
    for v in range(8):
        a, b, c, d = before[v], low[v], high[v], after[v]
        mid_low = rows(2, v) * b + 0.5 * (a + 2.0 * b + c) + 0.25 * (a + 4.0 * b + c)
        mid_high = rows(3, v) * c + 0.5 * (b + 2.0 * c + d) + 0.25 * (b + 4.0 * c + d)
        sub[v] = (0.25 * a, -(a + b), zero, 0.25 * b)
        diag[v] = (mid_low, -(b + c), -(b + c), mid_high)
        sup[v] = (0.25 * c, zero, -(c + d), 0.25 * d)
    sub[0] = tuple(jnp.where(plane == 0, 0.0, m) for m in sub[0])
    sup[7] = tuple(jnp.where(plane == 7, 0.0, m) for m in sup[7])
    count = [0]

    def keep(members):
        for m in members:
            fac_ref[count[0]] = m
            count[0] += 1

    inverse = {}
    for e, o, n, wraps in STEPS:
        for x in (e, n):
            if x not in inverse:
                inverse[x] = mat_inv(diag[x])
        inv_n, sub_n, sup_n = inverse[n], sub[n], sup[n]
        if wraps:
            inv_n, sub_n, sup_n = rolled(inv_n, -1, 0), rolled(sub_n, -1, 0), rolled(sup_n, -1, 0)
        left = minus(mat_mat(sub[o], inverse[e]))
        right = minus(mat_mat(sup[o], inv_n))
        keep(left)
        keep(right)
        keep(inverse[e])
        keep(mat_mat(inverse[e], sub[e]))
        keep(mat_mat(inverse[e], sup[e]))
        sub[o] = mat_mat(left, sub[e])
        diag[o] = plus(diag[o], plus(mat_mat(left, sup[e]), mat_mat(right, sub_n)))
        sup[o] = mat_mat(right, sup_n)
    s, d, u = sub[7], diag[7], sup[7]
    for h in (1, 2, 4):
        inv = mat_inv(d)
        left = minus(mat_mat(s, rolled(inv, h, 0)))
        right = minus(mat_mat(u, rolled(inv, -h, 0)))
        keep(left)
        keep(right)
        s_low, u_low = rolled(s, h, 0), rolled(u, h, 0)
        s_high, u_high = rolled(s, -h, 0), rolled(u, -h, 0)
        d = plus(d, plus(mat_mat(left, u_low), mat_mat(right, s_high)))
        s, u = mat_mat(left, s_low), mat_mat(right, u_high)
    keep(mat_inv(d))


def substitute(fac_ref, side_ref, out_ref):
    def fac(first):
        return tuple(fac_ref[first + j][None] for j in range(4))

    r = [
        tuple(side_ref[:, c, 8 * v : 8 * v + 8, :] for c in range(2)) for v in range(8)
    ]
    at = 0
    bases = {}
    for e, o, n, wraps in STEPS:
        side_n = rolled(r[n], -1, 1) if wraps else r[n]
        r[o] = plus(r[o], plus(mat_vec(fac(at), r[e]), mat_vec(fac(at + 4), side_n)))
        bases[e] = at + 8
        at += 20
    x = r[7]
    for h in (1, 2, 4):
        x = plus(
            x,
            plus(mat_vec(fac(at), rolled(x, h, 1)), mat_vec(fac(at + 4), rolled(x, -h, 1))),
        )
        at += 8
    values = {7: mat_vec(fac(at), x)}
    for e in (3, 5, 1, 6, 4, 2, 0):
        base = bases[e]
        prior, wraps = BEFORE[e]
        low = rolled(values[prior], 1, 1) if wraps else values[prior]
        back = plus(mat_vec(fac(base + 4), low), mat_vec(fac(base + 8), values[AFTER[e]]))
        values[e] = tuple(a - b for a, b in zip(mat_vec(fac(base), r[e]), back))
    for v in range(8):
        for c in range(2):
            out_ref[:, c, 8 * v : 8 * v + 8, :] = values[v][c]


def invert_lines(next_ref, prev_ref):
    lane = lax.broadcasted_iota(jnp.int32, (CHUNKS, LANES), 1).astype(F32)
    chunk = lax.broadcasted_iota(jnp.int32, (CHUNKS, LANES), 0)
    slot = lax.broadcasted_iota(jnp.int32, (LANES, LANES), 0)

    def body(q, total):
        row = next_ref[pl.ds(q, 1), :]
        hit = jnp.broadcast_to(row >> 7, (CHUNKS, LANES)) == chunk
        place = jnp.where(jnp.broadcast_to(row & 127, (LANES, LANES)) == slot, 1.0, 0.0)
        left = jnp.concatenate([jnp.where(hit, lane, 0.0), jnp.where(hit, 1.0, 0.0)], axis=0)
        found = lax.dot_general(
            left.astype(jnp.bfloat16),
            place.astype(jnp.bfloat16),
            (((1,), (1,)), ((), ())),
            preferred_element_type=F32,
        )
        return total + found[:CHUNKS] + found[CHUNKS:] * (q.astype(F32) * 128.0)

    total = lax.fori_loop(0, CHUNKS, body, jnp.zeros((CHUNKS, LANES), F32))
    prev_ref[...] = total.astype(jnp.int32)


def gather_lines(source, target, index_ref):
    source_rows = source.reshape(24 * CHUNKS, LANES)
    target_rows = target.reshape(24 * CHUNKS, LANES)

    def body(c, carry):
        row = jnp.broadcast_to(index_ref[pl.ds(c, 1), :], (8, LANES))
        lane = row & 127
        chunk = row >> 7
        found = [jnp.zeros((8, LANES), F32) for _ in range(3)]
        for s in range(CHUNKS):
            hit = chunk == s
            for g in range(3):
                rows = source_rows[pl.ds(g * 8 * CHUNKS + s, 8, stride=CHUNKS), :]
                found[g] = jnp.where(hit, jnp.take_along_axis(rows, lane, axis=1), found[g])
        for g in range(3):
            target_rows[pl.ds(g * 8 * CHUNKS + c, 8, stride=CHUNKS), :] = found[g]
        return carry

    lax.fori_loop(0, CHUNKS, body, 0)


def tell_depths(sem, me, depth, distance):
    @pl.when(depth >= distance)
    def _():
        pl.semaphore_signal(sem, 1, device_id={"cell": me - 8 * distance})

    @pl.when(depth < 8 - distance)
    def _():
        pl.semaphore_signal(sem, 1, device_id={"cell": me + 8 * distance})


def depth_peers(depth, distance):
    return jnp.where(depth >= distance, 1, 0) + jnp.where(depth < 8 - distance, 1, 0)


def kernel(
    state_ref, rate_ref, next_ref, codes_ref, out_ref,
    own, low, high, other, shifted, kflux, kprev, rhs, lp, prev, codes, coef, fac, side, delta,
    load_sem, ghost_sem, inst_sem, coef_sem, side_sem, back_sem, self_sem, known,
):
    me = lax.axis_index("cell")
    inst = lax.axis_index("inst")
    barrier = pltpu.get_barrier_semaphore()

    depth = me >> 3
    for j in range(1, 4):
        pl.semaphore_signal(barrier, 1, device_id={"inst": inst ^ j})
    for j in range(1, 5):
        pl.semaphore_signal(barrier, 1, device_id={"cell": me ^ j})
    tell_depths(barrier, me, depth, 1)

    loads = [
        pltpu.make_async_copy(state_ref.at[:, :, :, c], own.at[:, :, c], load_sem.at[c])
        for c in range(2)
    ] + [
        pltpu.make_async_copy(rate_ref.at[:, c], lp.at[i, 2 + c], load_sem.at[2 + 2 * i + c])
        for i in range(2)
        for c in range(2)
    ]
    for copy in loads:
        copy.start()
    invert_lines(next_ref, prev)
    codes[...] = jnp.zeros((8, LANES), jnp.int32)
    codes[0:2, 0:64] = codes_ref[...]
    for copy in loads:
        copy.wait()

    def own_radius(i, carry):
        for c in range(2):
            vel_x, _, _, sound = primitives([own[i, v, c] for v in range(6)])
            lp[i, c] = jnp.abs(vel_x) + sound
        return carry

    def pitch_flux(i, carry):
        for c in range(2):
            here = [own[i, v, c] for v in range(6)]
            there = [shifted[i, v, c] for v in range(6)]
            _, vel_h, p_h, sound_h = primitives(here)
            _, vel_t, p_t, sound_t = primitives(there)
            flux_h = flux(here, vel_h, p_h, 2)
            flux_t = flux(there, vel_t, p_t, 2)
            radius = 0.25 * (jnp.abs(vel_h) + sound_h + jnp.abs(vel_t) + sound_t)
            for v in range(6):
                kflux[i, v, c] = 0.5 * (flux_h[v] + flux_t[v]) - radius * (there[v] - here[v])
        return carry

    pl.semaphore_wait(barrier, 7 + depth_peers(depth, 1))
    to_pair = pltpu.make_async_remote_copy(
        own, other.at[1], inst_sem.at[0], inst_sem.at[1], device_id={"inst": inst ^ 2}
    )
    to_pair.start()
    to_right = pltpu.make_async_remote_copy(
        own, low, ghost_sem.at[0], ghost_sem.at[1], device_id={"cell": lax.rem(me + 1, CELLS)}
    )
    to_left = pltpu.make_async_remote_copy(
        own, high, ghost_sem.at[2], ghost_sem.at[3], device_id={"cell": lax.rem(me + CELLS - 1, CELLS)}
    )
    row_start = (me & 3) == 0
    row_end = (me & 3) == 3
    first = me == 0
    last = me == CELLS - 1
    pl.when(jnp.logical_not(row_end))(to_right.start)
    pl.when(jnp.logical_not(row_start))(to_left.start)
    to_twin = pltpu.make_async_remote_copy(
        own, other.at[0], inst_sem.at[2], inst_sem.at[3], device_id={"inst": inst ^ 1}
    )
    to_twin.start()

    pl.semaphore_signal(known.at[0], 1, device_id={"cell": me ^ 4})
    pl.semaphore_wait(known.at[0], 1)
    tell_depths(known.at[1], me, depth, 1)
    pl.semaphore_wait(known.at[1], depth_peers(depth, 1))
    pl.when(jnp.logical_and(row_end, jnp.logical_not(last)))(to_right.start)
    pl.when(jnp.logical_and(row_start, jnp.logical_not(first)))(to_left.start)
    tell_depths(known.at[2], me, depth, 2)
    lax.fori_loop(0, 2, own_radius, 0)
    pl.semaphore_wait(known.at[2], depth_peers(depth, 2))
    pl.semaphore_signal(known.at[3], 1, device_id={"cell": me ^ 32})
    gather_lines(own, shifted, next_ref)
    lax.fori_loop(0, 2, pitch_flux, 0)
    pl.semaphore_wait(known.at[3], 1)

    my_row = (me & 7) * 8 + (me >> 3)

    def send_coef(j, carry):
        peer = lax.rem(me + j, CELLS)
        pltpu.make_async_remote_copy(
            lp.at[peer >> 5, :, peer & 15],
            coef.at[:, my_row],
            coef_sem.at[0],
            coef_sem.at[1],
            device_id={"cell": peer},
        ).start()
        return carry

    lax.fori_loop(1, CELLS, send_coef, 0)
    my_coef = pltpu.make_async_copy(lp.at[me >> 5, :, me & 15], coef.at[:, my_row], self_sem.at[0])
    my_coef.start()

    gather_lines(kflux, kprev, prev)

    to_pair.wait_recv()
    to_forward = pltpu.make_async_remote_copy(
        other.at[1], other.at[2], inst_sem.at[4], inst_sem.at[5], device_id={"inst": inst ^ 1}
    )
    to_forward.start()

    pltpu.make_async_copy(
        coef.at[:, pl.ds(0, CELLS - 1)], coef.at[:, pl.ds(0, CELLS - 1)], coef_sem.at[1]
    ).wait()
    my_coef.wait()
    factorise(coef, fac)

    pl.when(jnp.logical_not(first))(to_right.wait_recv)
    pl.when(jnp.logical_not(last))(to_left.wait_recv)
    spread = lax.broadcasted_iota(jnp.int32, (CHUNKS, LANES), 0) * 4 + (
        lax.broadcasted_iota(jnp.int32, (CHUNKS, LANES), 1) // TILE_LINES
    )
    end_codes = [
        jnp.take_along_axis(jnp.broadcast_to(codes[e : e + 1, :], (CHUNKS, LANES)), spread, axis=1)
        for e in range(2)
    ]

    @pl.when(first)
    def _():
        for i in range(2):
            near, far = ghost_cells(
                [own[i, v, 0] for v in range(6)], [own[i, v, 1] for v in range(6)], end_codes[0]
            )
            for v in range(6):
                low[i, v, 0] = far[v]
                low[i, v, 1] = near[v]

    @pl.when(last)
    def _():
        for i in range(2):
            near, far = ghost_cells(
                [own[i, v, 1] for v in range(6)], [own[i, v, 0] for v in range(6)], end_codes[1]
            )
            for v in range(6):
                high[i, v, 0] = near[v]
                high[i, v, 1] = far[v]

    def add_line(i, carry):
        cells = [[part[i, v, c] for v in range(6)] for part in (low, own, high) for c in range(2)]
        parts = line_part(cells)
        for c in range(2):
            for v in range(6):
                rhs[i, v, c] = kprev[i, v, c] - kflux[i, v, c] - parts[c][v]
        return carry

    lax.fori_loop(0, 2, add_line, 0)
    to_twin.wait_recv()
    to_forward.wait_recv()
    weights = [
        [[time_weight(inst, n, slot, m) for m in range(2)] for slot in range(4)] for n in range(2)
    ]

    def add_time(v, carry):
        for c in range(2):
            planes = [[own[m, v, c] for m in range(2)]] + [
                [other[slot, m, v, c] for m in range(2)] for slot in range(3)
            ]
            for n in range(2):
                total = rhs[n, v, c]
                for slot in range(4):
                    for m in range(2):
                        if slot == 0 and m == n:
                            continue
                        total = total - weights[n][slot][m] * planes[slot][m]
                rhs[n, v, c] = total
        return carry

    lax.fori_loop(0, 6, add_time, 0)

    def send_side(j, carry):
        peer = lax.rem(me + j, CELLS)
        pltpu.make_async_remote_copy(
            rhs.at[peer >> 5, pl.ds(((peer >> 4) & 1) * 3, 3), :, peer & 15],
            side.at[:, :, my_row],
            side_sem.at[0],
            side_sem.at[1],
            device_id={"cell": peer},
        ).start()
        return carry

    lax.fori_loop(1, CELLS, send_side, 0)
    my_inst, my_var, my_chunk = me >> 5, ((me >> 4) & 1) * 3, me & 15
    my_side = pltpu.make_async_copy(
        rhs.at[my_inst, pl.ds(my_var, 3), :, my_chunk], side.at[:, :, my_row], self_sem.at[1]
    )
    my_side.start()
    many = side.at[:, :, pl.ds(0, CELLS - 1)]
    pltpu.make_async_copy(many, many, side_sem.at[1]).wait()
    my_side.wait()
    substitute(fac, side, delta)

    def send_back(j, carry):
        peer = lax.rem(me + j, CELLS)
        pltpu.make_async_remote_copy(
            delta.at[:, :, (peer & 7) * 8 + (peer >> 3)],
            out_ref.at[my_inst, pl.ds(my_var, 3), my_chunk],
            back_sem.at[0],
            back_sem.at[1],
            device_id={"cell": peer},
        ).start()
        return carry

    lax.fori_loop(1, CELLS, send_back, 0)
    my_back = pltpu.make_async_copy(
        delta.at[:, :, my_row], out_ref.at[my_inst, pl.ds(my_var, 3), my_chunk], self_sem.at[2]
    )
    my_back.start()
    for copy in (to_pair, to_twin, to_forward):
        copy.wait_send()
    pl.when(jnp.logical_not(last))(to_right.wait_send)
    pl.when(jnp.logical_not(first))(to_left.wait_send)
    few = coef.at[:, pl.ds(0, CELLS - 1)]
    pltpu.make_async_copy(few, few, coef_sem.at[0]).wait()
    pltpu.make_async_copy(many, many, side_sem.at[0]).wait()
    pltpu.make_async_copy(many, many, back_sem.at[0]).wait()
    pltpu.make_async_copy(many, many, back_sem.at[1]).wait()
    my_back.wait()


def local(state, pseudo_rate, line_next, face_codes):
    view = state.reshape(2, 6, 2, CHUNKS, LANES).transpose(0, 1, 3, 2, 4)
    rate = pseudo_rate.reshape(2, CHUNKS, LANES).transpose(1, 0, 2)
    block = (2, 6, 2, CHUNKS, LANES)
    in_vmem = pl.BlockSpec(memory_space=pltpu.VMEM)
    in_place = pl.BlockSpec(memory_space=pl.ANY)
    dma = pltpu.SemaphoreType.DMA
    update = pl.pallas_call(
        kernel,
        out_shape=jax.ShapeDtypeStruct((2, 6, CHUNKS, 2, LANES), F32),
        in_specs=[in_place, in_place, in_vmem, in_vmem],
        out_specs=in_vmem,
        scratch_shapes=[
            pltpu.VMEM(block, F32),
            pltpu.VMEM(block, F32),
            pltpu.VMEM(block, F32),
            pltpu.VMEM((3,) + block, F32),
            pltpu.VMEM(block, F32),
            pltpu.VMEM(block, F32),
            pltpu.VMEM(block, F32),
            pltpu.VMEM(block, F32),
            pltpu.VMEM((2, 4, CHUNKS, LANES), F32),
            pltpu.VMEM((CHUNKS, LANES), jnp.int32),
            pltpu.VMEM((8, LANES), jnp.int32),
            pltpu.VMEM((4, CELLS, LANES), F32),
            pltpu.VMEM((FACTOR_PLANES, 8, LANES), F32),
            pltpu.VMEM((3, 2, CELLS, LANES), F32),
            pltpu.VMEM((3, 2, CELLS, LANES), F32),
            dma((6,)),
            dma((4,)),
            dma((6,)),
            dma((2,)),
            dma((2,)),
            dma((2,)),
            dma((3,)),
            pltpu.SemaphoreType.REGULAR((4,)),
        ],
        compiler_params=pltpu.CompilerParams(collective_id=0, has_side_effects=True),
        name="line_implicit_step",
    )(view, rate, line_next.reshape(CHUNKS, LANES), face_codes)
    return state + update.transpose(0, 1, 3, 2, 4).reshape(state.shape)


def solution(mesh):
    placed = (P("inst", None, "cell", None), P("cell", None), P(), P())
    return jax.shard_map(
        local, mesh=mesh, in_specs=placed, out_specs=P("inst", None, "cell", None), check_vma=False
    )
```

```python
import jax
import jax.numpy as jnp
import numpy as np
from jax import lax
from jax.experimental import pallas as pl
from jax.experimental.pallas import tpu as pltpu
from jax.sharding import PartitionSpec as P

NT = 8
CELLS = 64
CHUNKS = 16
LANES = 128
HALF = 64
TILE_LINES = 32
GAMMA_GAS = 1.4
FREE_STATE = (1.0, 0.5, 0.0, 0.0, 2.625, 0.2)
F32 = jnp.float32
FACTOR_PLANES = 84


def spectral_table():
    offsets = np.arange(NT)[:, None] - np.arange(NT)[None, :]
    angles = np.pi * offsets / NT
    safe_sin = np.where(offsets == 0, 1.0, np.sin(angles))
    parity = np.where(np.mod(offsets, 2) == 0, -1.0, 1.0)
    return np.where(offsets == 0, 0.0, 0.5 * parity * np.cos(angles) / safe_sin)


def time_weight(inst, row, slot, column):
    table = spectral_table()
    values = [float(table[2 * i + row, 2 * (i ^ slot) + column]) for i in range(NT // 2)]
    weight = jnp.float32(values[3])
    for i in (2, 1, 0):
        weight = jnp.where(inst == i, jnp.float32(values[i]), weight)
    return weight


def primitives(cell):
    inverse = 1.0 / cell[0]
    vel_x = cell[1] * inverse
    vel_y = cell[2] * inverse
    vel_z = cell[3] * inverse
    pressure = 0.4 * (cell[4] - 0.5 * cell[0] * (vel_x * vel_x + vel_y * vel_y + vel_z * vel_z))
    sound = jnp.sqrt(GAMMA_GAS * pressure * inverse)
    return vel_x, vel_y, pressure, sound


def flux(cell, velocity, pressure, component):
    rows = [cell[v] * velocity for v in range(6)]
    rows[component] = rows[component] + pressure
    rows[4] = rows[4] + pressure * velocity
    return rows


def swap(x):
    return pltpu.roll(x, HALF, x.ndim - 1)


def low_lanes(shape):
    return lax.broadcasted_iota(jnp.int32, shape, len(shape) - 1) < HALF


def pack(cell_a, cell_b):
    low = low_lanes(cell_a.shape)
    return jnp.where(low, cell_a, swap(cell_b)), jnp.where(low, swap(cell_a), cell_b)


def following(planes, swapped, p):
    low = low_lanes((8, LANES))
    return jnp.where(low, swapped[p], swapped[min(p + 1, len(planes) - 1)])


def preceding(planes, swapped, p):
    low = low_lanes((8, LANES))
    return jnp.where(low, swapped[max(p - 1, 0)], swapped[p])


def line_terms(state_ref, codes, line_ref):
    low = low_lanes((8, LANES))
    plane = lax.broadcasted_iota(jnp.int32, (8, LANES), 0)
    cells = []
    for v in range(6):
        inner = [state_ref[v, 8 * p : 8 * p + 8, :] for p in range(8)]
        ends = []
        for block, code, keep_low in ((inner[0], codes[0], True), (inner[7], codes[1], False)):
            turned = swap(block)
            mirror = -turned if v == 1 else turned
            copied = jnp.where(low, block, turned) if keep_low else jnp.where(low, turned, block)
            inflow = jnp.full((8, LANES), FREE_STATE[v], F32)
            ends.append(jnp.where(code == 0, mirror, jnp.where(code == 1, inflow, copied)))
        before = jnp.where(plane == 0, ends[0], pltpu.roll(inner[7], 1, 0))
        after = jnp.where(plane == 7, ends[1], pltpu.roll(inner[0], 7, 0))
        cells.append([before] + inner + [after])
    parts = [primitives([cells[v][p] for v in range(6)]) for p in range(10)]
    speed = [q[0] for q in parts]
    pressure = [q[2] for q in parts]
    radius = [jnp.abs(q[0]) + q[3] for q in parts]
    turned = [swap(q) for q in pressure]
    sensor = []
    for p in range(10):
        up, down = following(pressure, turned, p), preceding(pressure, turned, p)
        sensor.append(
            jnp.abs(up - 2.0 * pressure[p] + down) / (up + 2.0 * pressure[p] + down)
        )
    turned_sensor = [swap(q) for q in sensor]
    turned_radius = [swap(q) for q in radius]
    second, fourth, face_radius = [], [], []
    for p in range(9):
        e2 = 0.25 * jnp.maximum(sensor[p], following(sensor, turned_sensor, p))
        second.append(e2)
        fourth.append(jnp.maximum(0.0, 0.03125 - e2))
        face_radius.append(0.5 * (radius[p] + following(radius, turned_radius, p)))
    for v in range(6):
        own = cells[v]
        turned = [swap(q) for q in own]
        moved = [own[p] * speed[p] for p in range(10)]
        if v == 1:
            moved = [moved[p] + pressure[p] for p in range(10)]
        if v == 4:
            moved = [moved[p] + pressure[p] * speed[p] for p in range(10)]
        turned_moved = [swap(q) for q in moved]
        faces = []
        for p in range(9):
            near = following(own, turned, p) - own[p]
            far = own[p + 1] - preceding(own, turned, p) - 3.0 * near
            faces.append(
                0.5 * (moved[p] + following(moved, turned_moved, p))
                - face_radius[p] * (second[p] * near - fourth[p] * far)
            )
        turned_faces = [swap(q) for q in faces]
        for p in range(8):
            line_ref[v, 8 * p : 8 * p + 8, :] = faces[p + 1] - preceding(
                faces, turned_faces, p + 1
            )
    return radius


def mat_mat(a, b):
    return a[0] * b[0] + a[1] * swap(b[1]), a[0] * b[1] + a[1] * swap(b[0])


def mat_vec(a, x):
    return a[0] * x + a[1] * swap(x)


def mat_inv(m):
    turned = swap(m[0])
    reciprocal = 1.0 / (m[0] * turned - m[1] * swap(m[1]))
    return turned * reciprocal, -m[1] * reciprocal


def plus(a, b):
    return tuple(x + y for x, y in zip(a, b))


def minus(a):
    return tuple(-x for x in a)


def rolled(members, shift):
    return tuple(pltpu.roll(m, shift % 8, m.ndim - 2) for m in members)


STEPS = (
    (0, 1, 2, False),
    (2, 3, 4, False),
    (4, 5, 6, False),
    (6, 7, 0, True),
    (1, 3, 5, False),
    (5, 7, 1, True),
    (3, 7, 3, True),
)
BEFORE = {
    0: (7, True),
    2: (1, False),
    4: (3, False),
    6: (5, False),
    1: (7, True),
    5: (3, False),
    3: (7, True),
}
AFTER = {0: 1, 2: 3, 4: 5, 6: 7, 1: 3, 5: 7, 3: 7}


def factorise(radius, rate, fac_ref):
    low = low_lanes((8, LANES))
    plane = lax.broadcasted_iota(jnp.int32, (8, LANES), 0)
    radius = (
        [jnp.where(plane == 0, 0.0, radius[0])]
        + radius[1:9]
        + [jnp.where(plane == 7, 0.0, radius[9])]
    )
    turned = [swap(q) for q in radius]
    sub, diag, sup = {}, {}, {}
    for p in range(8):
        b = radius[p + 1]
        a = preceding(radius, turned, p + 1)
        c = following(radius, turned, p + 1)
        lower, upper = -(a + b), -(b + c)
        middle = rate[p] * b + 0.5 * (a + 2.0 * b + c) + 0.25 * (a + 4.0 * b + c)
        sub[p] = (0.25 * a, jnp.where(low, lower, 0.0))
        diag[p] = (middle, jnp.where(low, upper, lower))
        sup[p] = (0.25 * c, jnp.where(low, 0.0, upper))
    sub[0] = tuple(jnp.where(plane == 0, 0.0, m) for m in sub[0])
    sup[7] = tuple(jnp.where(plane == 7, 0.0, m) for m in sup[7])
    count = [0]

    def keep(members):
        for m in members:
            fac_ref[count[0]] = m
            count[0] += 1

    inverse = {}
    for e, o, n, wraps in STEPS:
        for x in (e, n):
            if x not in inverse:
                inverse[x] = mat_inv(diag[x])
        inv_n, sub_n, sup_n = inverse[n], sub[n], sup[n]
        if wraps:
            inv_n, sub_n, sup_n = rolled(inv_n, -1), rolled(sub_n, -1), rolled(sup_n, -1)
        left = minus(mat_mat(sub[o], inverse[e]))
        right = minus(mat_mat(sup[o], inv_n))
        keep(left)
        keep(right)
        keep(inverse[e])
        keep(mat_mat(inverse[e], sub[e]))
        keep(mat_mat(inverse[e], sup[e]))
        sub[o] = mat_mat(left, sub[e])
        diag[o] = plus(diag[o], plus(mat_mat(left, sup[e]), mat_mat(right, sub_n)))
        sup[o] = mat_mat(right, sup_n)
    s, d, u = sub[7], diag[7], sup[7]
    for h in (1, 2, 4):
        inv = mat_inv(d)
        left = minus(mat_mat(s, rolled(inv, h)))
        right = minus(mat_mat(u, rolled(inv, -h)))
        keep(left)
        keep(right)
        s_low, u_low = rolled(s, h), rolled(u, h)
        s_high, u_high = rolled(s, -h), rolled(u, -h)
        d = plus(d, plus(mat_mat(left, u_low), mat_mat(right, s_high)))
        s, u = mat_mat(left, s_low), mat_mat(right, u_high)
    keep(mat_inv(d))


def substitute(fac_ref, side_ref, line_ref, out_ref):
    def fac(first):
        return fac_ref[first][None], fac_ref[first + 1][None]

    def shift(x, count):
        return pltpu.roll(x, count % 8, 1)

    r = [side_ref[:, 8 * p : 8 * p + 8, :] - line_ref[:, 8 * p : 8 * p + 8, :] for p in range(8)]
    at = 0
    bases = {}
    for e, o, n, wraps in STEPS:
        side_n = shift(r[n], -1) if wraps else r[n]
        r[o] = r[o] + (mat_vec(fac(at), r[e]) + mat_vec(fac(at + 2), side_n))
        bases[e] = at + 4
        at += 10
    x = r[7]
    for h in (1, 2, 4):
        x = x + (mat_vec(fac(at), shift(x, h)) + mat_vec(fac(at + 2), shift(x, -h)))
        at += 4
    values = {7: mat_vec(fac(at), x)}
    for e in (3, 5, 1, 6, 4, 2, 0):
        base = bases[e]
        prior, wraps = BEFORE[e]
        low = shift(values[prior], 1) if wraps else values[prior]
        back = mat_vec(fac(base + 2), low) + mat_vec(fac(base + 4), values[AFTER[e]])
        values[e] = mat_vec(fac(base), r[e]) - back
    for p in range(8):
        out_ref[:, 8 * p : 8 * p + 8, :] = values[p]


def invert_lines(next_ref, prev_ref):
    lane = lax.broadcasted_iota(jnp.int32, (CHUNKS, LANES), 1).astype(F32)
    chunk = lax.broadcasted_iota(jnp.int32, (CHUNKS, LANES), 0)
    slot = lax.broadcasted_iota(jnp.int32, (LANES, LANES), 0)
    total = jnp.zeros((CHUNKS, LANES), F32)
    for q in range(CHUNKS):
        row = next_ref[q : q + 1, :]
        hit = jnp.broadcast_to(row >> 7, (CHUNKS, LANES)) == chunk
        place = jnp.where(jnp.broadcast_to(row & 127, (LANES, LANES)) == slot, 1.0, 0.0)
        left = jnp.concatenate([jnp.where(hit, lane, 0.0), jnp.where(hit, 1.0, 0.0)], axis=0)
        found = lax.dot_general(
            left.astype(jnp.bfloat16),
            place.astype(jnp.bfloat16),
            (((1,), (1,)), ((), ())),
            preferred_element_type=F32,
        )
        total = total + (found[:CHUNKS] + found[CHUNKS:] * (q * 128.0))
    prev_ref[...] = total.astype(jnp.int32)


def gather_lines(source, target, index_ref):
    source_rows = source.reshape(24 * CHUNKS, LANES)
    target_rows = target.reshape(24 * CHUNKS, LANES)

    def body(c, carry):
        row = jnp.broadcast_to(index_ref[pl.ds(c, 1), :], (8, LANES))
        lane = row & 127
        chunk = row >> 7
        found = [jnp.zeros((8, LANES), F32) for _ in range(3)]
        for s in range(CHUNKS):
            hit = chunk == s
            for g in range(3):
                rows = source_rows[pl.ds(g * 8 * CHUNKS + s, 8, stride=CHUNKS), :]
                found[g] = jnp.where(hit, jnp.take_along_axis(rows, lane, axis=1), found[g])
        for g in range(3):
            target_rows[pl.ds(g * 8 * CHUNKS + c, 8, stride=CHUNKS), :] = found[g]
        return carry

    lax.fori_loop(0, CHUNKS, body, 0)


def tell_depths(sem, me, depth, distance):
    @pl.when(depth >= distance)
    def _():
        pl.semaphore_signal(sem, 1, device_id={"cell": me - 8 * distance})

    @pl.when(depth < 8 - distance)
    def _():
        pl.semaphore_signal(sem, 1, device_id={"cell": me + 8 * distance})


def depth_peers(depth, distance):
    return jnp.where(depth >= distance, 1, 0) + jnp.where(depth < 8 - distance, 1, 0)


def kernel(
    state_ref, rate_ref, next_ref, codes_ref, out_ref,
    own, other, shifted, kflux, kprev, rate, sent_state, sent_side, prev, codes,
    lines, side, line, fac, delta, back,
    load_sem, inst_sem, state_sem, side_sem, back_sem, self_sem, known,
):
    me = lax.axis_index("cell")
    inst = lax.axis_index("inst")
    depth = me >> 3

    barrier = pltpu.get_barrier_semaphore()
    for j in range(1, 4):
        pl.semaphore_signal(barrier, 1, device_id={"inst": inst ^ j})
    for j in range(1, 5):
        pl.semaphore_signal(barrier, 1, device_id={"cell": me ^ j})
    tell_depths(barrier, me, depth, 1)
    loads = [
        pltpu.make_async_copy(state_ref.at[:, :, :, c], own.at[:, :, c], load_sem.at[c])
        for c in range(2)
    ] + [
        pltpu.make_async_copy(rate_ref.at[:, c], rate.at[c], load_sem.at[2 + c]) for c in range(2)
    ]
    for copy in loads:
        copy.start()
    pl.semaphore_wait(barrier, 7 + depth_peers(depth, 1))
    pl.semaphore_signal(known.at[0], 1, device_id={"cell": me ^ 4})
    for copy in loads:
        copy.wait()

    to_pair = [
        pltpu.make_async_remote_copy(
            own.at[i],
            other.at[1, i],
            inst_sem.at[0, i],
            inst_sem.at[1, i],
            device_id={"inst": inst ^ 2},
        )
        for i in range(2)
    ]
    to_twin = pltpu.make_async_remote_copy(
        own, other.at[0], inst_sem.at[2, 0], inst_sem.at[2, 1], device_id={"inst": inst ^ 1}
    )
    to_forward = [
        pltpu.make_async_remote_copy(
            other.at[1, i],
            other.at[2, i],
            inst_sem.at[3, i],
            inst_sem.at[4, i],
            device_id={"inst": inst ^ 1},
        )
        for i in range(2)
    ]
    for copy in to_pair:
        copy.start()
    to_twin.start()

    invert_lines(next_ref, prev)
    pl.semaphore_wait(known.at[0], 1)
    tell_depths(known.at[1], me, depth, 1)
    rate_rows = pack(rate[0], rate[1])

    def pack_state(i, carry):
        for v in range(6):
            rows = pack(own[i, v, 0], own[i, v, 1])
            for half in range(2):
                sent_state[i, half, v] = rows[half]
        for half in range(2):
            sent_state[i, half, 6] = rate_rows[half]
        return carry

    lax.fori_loop(0, 2, pack_state, 0)
    pl.semaphore_wait(known.at[1], depth_peers(depth, 1))
    tell_depths(known.at[2], me, depth, 2)
    gather_lines(own, shifted, next_ref)
    pl.semaphore_wait(known.at[2], depth_peers(depth, 2))
    pl.semaphore_signal(known.at[3], 1, device_id={"cell": me ^ 32})

    def pitch_flux(i, carry):
        for c in range(2):
            here = [own[i, v, c] for v in range(6)]
            there = [shifted[i, v, c] for v in range(6)]
            _, vel_h, p_h, sound_h = primitives(here)
            _, vel_t, p_t, sound_t = primitives(there)
            flux_h = flux(here, vel_h, p_h, 2)
            flux_t = flux(there, vel_t, p_t, 2)
            radius = 0.25 * (jnp.abs(vel_h) + sound_h + jnp.abs(vel_t) + sound_t)
            for v in range(6):
                kflux[i, v, c] = 0.5 * (flux_h[v] + flux_t[v]) - radius * (there[v] - here[v])
        return carry

    lax.fori_loop(0, 2, pitch_flux, 0)
    gather_lines(kflux, kprev, prev)
    pl.semaphore_wait(known.at[3], 1)

    my_row = (me & 7) * 8 + (me >> 3)
    my_inst, my_half, my_chunk = me >> 5, (me >> 4) & 1, me & 15

    def send_state(j, carry):
        peer = lax.rem(me + j, CELLS)
        pltpu.make_async_remote_copy(
            sent_state.at[peer >> 5, (peer >> 4) & 1, :, peer & 15],
            lines.at[:, my_row],
            state_sem.at[0],
            state_sem.at[1],
            device_id={"cell": peer},
        ).start()
        return carry

    lax.fori_loop(1, CELLS, send_state, 0)
    my_state = pltpu.make_async_copy(
        sent_state.at[my_inst, my_half, :, my_chunk], lines.at[:, my_row], self_sem.at[0]
    )
    my_state.start()

    weights = [
        [[time_weight(inst, n, slot, m) for m in range(2)] for slot in range(4)] for n in range(2)
    ]
    for i in range(2):
        to_pair[i].wait_recv()
        to_forward[i].start()
    to_twin.wait_recv()
    for copy in to_forward:
        copy.wait_recv()

    def add_time(v, carry):
        totals = [[None, None], [None, None]]
        for c in range(2):
            planes = [[own[m, v, c] for m in range(2)]] + [
                [other[slot, m, v, c] for m in range(2)] for slot in range(3)
            ]
            for n in range(2):
                total = kprev[n, v, c] - kflux[n, v, c]
                for slot in range(4):
                    for m in range(2):
                        if slot == 0 and m == n:
                            continue
                        total = total - weights[n][slot][m] * planes[slot][m]
                totals[n][c] = total
        for n in range(2):
            rows = pack(totals[n][0], totals[n][1])
            for half in range(2):
                sent_side[n, half, v] = rows[half]
        return carry

    lax.fori_loop(0, 6, add_time, 0)

    def send_side(j, carry):
        peer = lax.rem(me + j, CELLS)
        pltpu.make_async_remote_copy(
            sent_side.at[peer >> 5, (peer >> 4) & 1, :, peer & 15],
            side.at[:, my_row],
            side_sem.at[0],
            side_sem.at[1],
            device_id={"cell": peer},
        ).start()
        return carry

    lax.fori_loop(1, CELLS, send_side, 0)
    my_side = pltpu.make_async_copy(
        sent_side.at[my_inst, my_half, :, my_chunk], side.at[:, my_row], self_sem.at[1]
    )
    my_side.start()

    codes[...] = jnp.zeros((8, LANES), jnp.int32)
    codes[0:2, 0:64] = codes_ref[...]
    lane = lax.broadcasted_iota(jnp.int32, (8, LANES), 1)
    tile = my_chunk * 4 + my_half * 2 + ((lane & (HALF - 1)) >> 5)
    end_codes = [
        jnp.take_along_axis(jnp.broadcast_to(codes[e : e + 1, :], (8, LANES)), tile, axis=1)
        for e in range(2)
    ]
    many = lines.at[:, pl.ds(0, CELLS - 1)]
    pltpu.make_async_copy(many, many, state_sem.at[1]).wait()
    my_state.wait()
    radius = line_terms(lines, end_codes, line)
    factorise(radius, [lines[6, 8 * p : 8 * p + 8, :] for p in range(8)], fac)
    few = side.at[:, pl.ds(0, CELLS - 1)]
    pltpu.make_async_copy(few, few, side_sem.at[1]).wait()
    my_side.wait()
    substitute(fac, side, line, delta)

    def send_back(j, carry):
        peer = lax.rem(me + j, CELLS)
        pltpu.make_async_remote_copy(
            delta.at[:, (peer & 7) * 8 + (peer >> 3)],
            back.at[my_inst, my_half, :, my_chunk],
            back_sem.at[0],
            back_sem.at[1],
            device_id={"cell": peer},
        ).start()
        return carry

    lax.fori_loop(1, CELLS, send_back, 0)
    my_back = pltpu.make_async_copy(
        delta.at[:, my_row], back.at[my_inst, my_half, :, my_chunk], self_sem.at[2]
    )
    my_back.start()
    for copy in (*to_pair, to_twin, *to_forward):
        copy.wait_send()
    pltpu.make_async_copy(many, many, state_sem.at[0]).wait()
    pltpu.make_async_copy(few, few, side_sem.at[0]).wait()
    pltpu.make_async_copy(few, few, back_sem.at[0]).wait()
    pltpu.make_async_copy(few, few, back_sem.at[1]).wait()
    my_back.wait()

    def finish(i, carry):
        for v in range(6):
            update = pack(back[i, 0, v], back[i, 1, v])
            for c in range(2):
                out_ref[pl.ds((i * 6 + v) * 2 * CHUNKS + c, CHUNKS, stride=2), :] = (
                    own[i, v, c] + update[c]
                )
        return carry

    lax.fori_loop(0, 2, finish, 0)


def local(state, pseudo_rate, line_next, face_codes):
    view = state.reshape(2, 6, 2, CHUNKS, LANES).transpose(0, 1, 3, 2, 4)
    rate = pseudo_rate.reshape(2, CHUNKS, LANES).transpose(1, 0, 2)
    block = (2, 6, 2, CHUNKS, LANES)
    in_vmem = pl.BlockSpec(memory_space=pltpu.VMEM)
    in_place = pl.BlockSpec(memory_space=pl.ANY)
    dma = pltpu.SemaphoreType.DMA
    rows = pl.pallas_call(
        kernel,
        out_shape=jax.ShapeDtypeStruct((2 * 6 * CHUNKS * 2, LANES), F32),
        in_specs=[in_place, in_place, in_vmem, in_vmem],
        out_specs=in_vmem,
        scratch_shapes=[
            pltpu.VMEM(block, F32),
            pltpu.VMEM((3,) + block, F32),
            pltpu.VMEM(block, F32),
            pltpu.VMEM(block, F32),
            pltpu.VMEM(block, F32),
            pltpu.VMEM((2, CHUNKS, LANES), F32),
            pltpu.VMEM((2, 2, 7, CHUNKS, LANES), F32),
            pltpu.VMEM((2, 2, 6, CHUNKS, LANES), F32),
            pltpu.VMEM((CHUNKS, LANES), jnp.int32),
            pltpu.VMEM((8, LANES), jnp.int32),
            pltpu.VMEM((7, CELLS, LANES), F32),
            pltpu.VMEM((6, CELLS, LANES), F32),
            pltpu.VMEM((6, CELLS, LANES), F32),
            pltpu.VMEM((FACTOR_PLANES, 8, LANES), F32),
            pltpu.VMEM((6, CELLS, LANES), F32),
            pltpu.VMEM((2, 2, 6, CHUNKS, LANES), F32),
            dma((4,)),
            dma((5, 2)),
            dma((2,)),
            dma((2,)),
            dma((2,)),
            dma((3,)),
            pltpu.SemaphoreType.REGULAR((4,)),
        ],
        compiler_params=pltpu.CompilerParams(collective_id=0, has_side_effects=True),
        name="line_implicit_step",
    )(view, rate, line_next.reshape(CHUNKS, LANES), face_codes)
    return rows.reshape(2, 6, CHUNKS, 2, LANES).transpose(0, 1, 3, 2, 4).reshape(state.shape)


def solution(mesh):
    placed = (P("inst", None, "cell", None), P("cell", None), P(), P())
    return jax.shard_map(
        local, mesh=mesh, in_specs=placed, out_specs=P("inst", None, "cell", None), check_vma=False
    )
```

```python
import jax
import jax.numpy as jnp
import numpy as np
from jax import lax
from jax.experimental import pallas as pl
from jax.experimental.pallas import tpu as pltpu
from jax.sharding import PartitionSpec as P

NT = 8
CELLS = 64
CHUNKS = 16
LANES = 128
HALF = 64
TILE_LINES = 32
GAMMA_GAS = 1.4
FREE_STATE = (1.0, 0.5, 0.0, 0.0, 2.625, 0.2)
F32 = jnp.float32
FACTOR_PLANES = 84


def spectral_table():
    offsets = np.arange(NT)[:, None] - np.arange(NT)[None, :]
    angles = np.pi * offsets / NT
    safe_sin = np.where(offsets == 0, 1.0, np.sin(angles))
    parity = np.where(np.mod(offsets, 2) == 0, -1.0, 1.0)
    return np.where(offsets == 0, 0.0, 0.5 * parity * np.cos(angles) / safe_sin)


def time_weight(inst, row, slot, column):
    table = spectral_table()
    values = [float(table[2 * i + row, 2 * (i ^ slot) + column]) for i in range(NT // 2)]
    weight = jnp.float32(values[3])
    for i in (2, 1, 0):
        weight = jnp.where(inst == i, jnp.float32(values[i]), weight)
    return weight


def primitives(cell):
    inverse = 1.0 / cell[0]
    vel_x = cell[1] * inverse
    vel_y = cell[2] * inverse
    vel_z = cell[3] * inverse
    pressure = 0.4 * (cell[4] - 0.5 * cell[0] * (vel_x * vel_x + vel_y * vel_y + vel_z * vel_z))
    sound = jnp.sqrt(GAMMA_GAS * pressure * inverse)
    return vel_x, vel_y, pressure, sound


def flux(cell, velocity, pressure, component):
    rows = [cell[v] * velocity for v in range(6)]
    rows[component] = rows[component] + pressure
    rows[4] = rows[4] + pressure * velocity
    return rows


def swap(x):
    return pltpu.roll(x, HALF, x.ndim - 1)


def low_lanes(shape):
    return lax.broadcasted_iota(jnp.int32, shape, len(shape) - 1) < HALF


def pack(cell_a, cell_b):
    low = low_lanes(cell_a.shape)
    return jnp.where(low, cell_a, swap(cell_b)), jnp.where(low, swap(cell_a), cell_b)


def following(planes, swapped, p):
    low = low_lanes((8, LANES))
    return jnp.where(low, swapped[p], swapped[min(p + 1, len(planes) - 1)])


def preceding(planes, swapped, p):
    low = low_lanes((8, LANES))
    return jnp.where(low, swapped[max(p - 1, 0)], swapped[p])


def line_terms(state_ref, codes, line_ref):
    low = low_lanes((8, LANES))
    plane = lax.broadcasted_iota(jnp.int32, (8, LANES), 0)
    cells = []
    for v in range(6):
        inner = [state_ref[v, 8 * p : 8 * p + 8, :] for p in range(8)]
        ends = []
        for block, code, keep_low in ((inner[0], codes[0], True), (inner[7], codes[1], False)):
            turned = swap(block)
            mirror = -turned if v == 1 else turned
            copied = jnp.where(low, block, turned) if keep_low else jnp.where(low, turned, block)
            inflow = jnp.full((8, LANES), FREE_STATE[v], F32)
            ends.append(jnp.where(code == 0, mirror, jnp.where(code == 1, inflow, copied)))
        before = jnp.where(plane == 0, ends[0], pltpu.roll(inner[7], 1, 0))
        after = jnp.where(plane == 7, ends[1], pltpu.roll(inner[0], 7, 0))
        cells.append([before] + inner + [after])
    parts = [primitives([cells[v][p] for v in range(6)]) for p in range(10)]
    speed = [q[0] for q in parts]
    pressure = [q[2] for q in parts]
    radius = [jnp.abs(q[0]) + q[3] for q in parts]
    turned = [swap(q) for q in pressure]
    sensor = []
    for p in range(10):
        up, down = following(pressure, turned, p), preceding(pressure, turned, p)
        sensor.append(
            jnp.abs(up - 2.0 * pressure[p] + down) / (up + 2.0 * pressure[p] + down)
        )
    turned_sensor = [swap(q) for q in sensor]
    turned_radius = [swap(q) for q in radius]
    second, fourth, face_radius = [], [], []
    for p in range(9):
        e2 = 0.25 * jnp.maximum(sensor[p], following(sensor, turned_sensor, p))
        second.append(e2)
        fourth.append(jnp.maximum(0.0, 0.03125 - e2))
        face_radius.append(0.5 * (radius[p] + following(radius, turned_radius, p)))
    for v in range(6):
        own = cells[v]
        turned = [swap(q) for q in own]
        moved = [own[p] * speed[p] for p in range(10)]
        if v == 1:
            moved = [moved[p] + pressure[p] for p in range(10)]
        if v == 4:
            moved = [moved[p] + pressure[p] * speed[p] for p in range(10)]
        turned_moved = [swap(q) for q in moved]
        faces = []
        for p in range(9):
            near = following(own, turned, p) - own[p]
            far = own[p + 1] - preceding(own, turned, p) - 3.0 * near
            faces.append(
                0.5 * (moved[p] + following(moved, turned_moved, p))
                - face_radius[p] * (second[p] * near - fourth[p] * far)
            )
        turned_faces = [swap(q) for q in faces]
        for p in range(8):
            line_ref[v, 8 * p : 8 * p + 8, :] = faces[p + 1] - preceding(
                faces, turned_faces, p + 1
            )
    return radius


def mat_mat(a, b):
    return a[0] * b[0] + a[1] * swap(b[1]), a[0] * b[1] + a[1] * swap(b[0])


def mat_vec(a, x):
    return a[0] * x + a[1] * swap(x)


def mat_inv(m):
    turned = swap(m[0])
    reciprocal = 1.0 / (m[0] * turned - m[1] * swap(m[1]))
    return turned * reciprocal, -m[1] * reciprocal


def plus(a, b):
    return tuple(x + y for x, y in zip(a, b))


def minus(a):
    return tuple(-x for x in a)


def rolled(members, shift):
    return tuple(pltpu.roll(m, shift % 8, m.ndim - 2) for m in members)


STEPS = (
    (0, 1, 2, False),
    (2, 3, 4, False),
    (4, 5, 6, False),
    (6, 7, 0, True),
    (1, 3, 5, False),
    (5, 7, 1, True),
    (3, 7, 3, True),
)
BEFORE = {
    0: (7, True),
    2: (1, False),
    4: (3, False),
    6: (5, False),
    1: (7, True),
    5: (3, False),
    3: (7, True),
}
AFTER = {0: 1, 2: 3, 4: 5, 6: 7, 1: 3, 5: 7, 3: 7}


def factorise(radius, rate, fac_ref):
    low = low_lanes((8, LANES))
    plane = lax.broadcasted_iota(jnp.int32, (8, LANES), 0)
    radius = (
        [jnp.where(plane == 0, 0.0, radius[0])]
        + radius[1:9]
        + [jnp.where(plane == 7, 0.0, radius[9])]
    )
    turned = [swap(q) for q in radius]
    sub, diag, sup = {}, {}, {}
    for p in range(8):
        b = radius[p + 1]
        a = preceding(radius, turned, p + 1)
        c = following(radius, turned, p + 1)
        lower, upper = -(a + b), -(b + c)
        middle = rate[p] * b + 0.5 * (a + 2.0 * b + c) + 0.25 * (a + 4.0 * b + c)
        sub[p] = (0.25 * a, jnp.where(low, lower, 0.0))
        diag[p] = (middle, jnp.where(low, upper, lower))
        sup[p] = (0.25 * c, jnp.where(low, 0.0, upper))
    sub[0] = tuple(jnp.where(plane == 0, 0.0, m) for m in sub[0])
    sup[7] = tuple(jnp.where(plane == 7, 0.0, m) for m in sup[7])
    count = [0]

    def keep(members):
        for m in members:
            fac_ref[count[0]] = m
            count[0] += 1

    inverse = {}
    for e, o, n, wraps in STEPS:
        for x in (e, n):
            if x not in inverse:
                inverse[x] = mat_inv(diag[x])
        inv_n, sub_n, sup_n = inverse[n], sub[n], sup[n]
        if wraps:
            inv_n, sub_n, sup_n = rolled(inv_n, -1), rolled(sub_n, -1), rolled(sup_n, -1)
        left = minus(mat_mat(sub[o], inverse[e]))
        right = minus(mat_mat(sup[o], inv_n))
        keep(left)
        keep(right)
        keep(inverse[e])
        keep(mat_mat(inverse[e], sub[e]))
        keep(mat_mat(inverse[e], sup[e]))
        sub[o] = mat_mat(left, sub[e])
        diag[o] = plus(diag[o], plus(mat_mat(left, sup[e]), mat_mat(right, sub_n)))
        sup[o] = mat_mat(right, sup_n)
    s, d, u = sub[7], diag[7], sup[7]
    for h in (1, 2, 4):
        inv = mat_inv(d)
        left = minus(mat_mat(s, rolled(inv, h)))
        right = minus(mat_mat(u, rolled(inv, -h)))
        keep(left)
        keep(right)
        s_low, u_low = rolled(s, h), rolled(u, h)
        s_high, u_high = rolled(s, -h), rolled(u, -h)
        d = plus(d, plus(mat_mat(left, u_low), mat_mat(right, s_high)))
        s, u = mat_mat(left, s_low), mat_mat(right, u_high)
    keep(mat_inv(d))


def substitute(fac_ref, side_ref, line_ref, out_ref):
    def fac(first):
        return fac_ref[first][None], fac_ref[first + 1][None]

    def shift(x, count):
        return pltpu.roll(x, count % 8, 1)

    r = [side_ref[:, 8 * p : 8 * p + 8, :] - line_ref[:, 8 * p : 8 * p + 8, :] for p in range(8)]
    at = 0
    bases = {}
    for e, o, n, wraps in STEPS:
        side_n = shift(r[n], -1) if wraps else r[n]
        r[o] = r[o] + (mat_vec(fac(at), r[e]) + mat_vec(fac(at + 2), side_n))
        bases[e] = at + 4
        at += 10
    x = r[7]
    for h in (1, 2, 4):
        x = x + (mat_vec(fac(at), shift(x, h)) + mat_vec(fac(at + 2), shift(x, -h)))
        at += 4
    values = {7: mat_vec(fac(at), x)}
    for e in (3, 5, 1, 6, 4, 2, 0):
        base = bases[e]
        prior, wraps = BEFORE[e]
        low = shift(values[prior], 1) if wraps else values[prior]
        back = mat_vec(fac(base + 2), low) + mat_vec(fac(base + 4), values[AFTER[e]])
        values[e] = mat_vec(fac(base), r[e]) - back
    for p in range(8):
        out_ref[:, 8 * p : 8 * p + 8, :] = values[p]


def invert_lines(next_ref, prev_ref):
    lane = lax.broadcasted_iota(jnp.int32, (CHUNKS, LANES), 1).astype(F32)
    chunk = lax.broadcasted_iota(jnp.int32, (CHUNKS, LANES), 0)
    slot = lax.broadcasted_iota(jnp.int32, (LANES, LANES), 0)
    total = jnp.zeros((CHUNKS, LANES), F32)
    for q in range(CHUNKS):
        row = next_ref[q : q + 1, :]
        hit = jnp.broadcast_to(row >> 7, (CHUNKS, LANES)) == chunk
        place = jnp.where(jnp.broadcast_to(row & 127, (LANES, LANES)) == slot, 1.0, 0.0)
        left = jnp.concatenate([jnp.where(hit, lane, 0.0), jnp.where(hit, 1.0, 0.0)], axis=0)
        found = lax.dot_general(
            left.astype(jnp.bfloat16),
            place.astype(jnp.bfloat16),
            (((1,), (1,)), ((), ())),
            preferred_element_type=F32,
        )
        total = total + (found[:CHUNKS] + found[CHUNKS:] * (q * 128.0))
    prev_ref[...] = total.astype(jnp.int32)


def gather_lines(source, target, index_ref):
    source_rows = source.reshape(24 * CHUNKS, LANES)
    target_rows = target.reshape(24 * CHUNKS, LANES)

    def body(c, carry):
        row = jnp.broadcast_to(index_ref[pl.ds(c, 1), :], (8, LANES))
        lane = row & 127
        chunk = row >> 7
        found = [jnp.zeros((8, LANES), F32) for _ in range(3)]
        for s in range(CHUNKS):
            hit = chunk == s
            for g in range(3):
                rows = source_rows[pl.ds(g * 8 * CHUNKS + s, 8, stride=CHUNKS), :]
                found[g] = jnp.where(hit, jnp.take_along_axis(rows, lane, axis=1), found[g])
        for g in range(3):
            target_rows[pl.ds(g * 8 * CHUNKS + c, 8, stride=CHUNKS), :] = found[g]
        return carry

    lax.fori_loop(0, CHUNKS, body, 0)


def tell_depths(sem, me, depth, distance):
    @pl.when(depth >= distance)
    def _():
        pl.semaphore_signal(sem, 1, device_id={"cell": me - 8 * distance})

    @pl.when(depth < 8 - distance)
    def _():
        pl.semaphore_signal(sem, 1, device_id={"cell": me + 8 * distance})


def depth_peers(depth, distance):
    return jnp.where(depth >= distance, 1, 0) + jnp.where(depth < 8 - distance, 1, 0)


def farthest_first(me, send):
    for steps in ((4,), (3, 5), (2, 6), (1, 7), (0,)):

        def body(t, carry, steps=steps):
            for step in steps:
                send(lax.rem(me + 8 * step, CELLS) ^ (7 - t))
            return carry

        lax.fori_loop(0, 8 if steps[0] else 7, body, 0)


def kernel(
    state_ref, rate_ref, next_ref, codes_ref, out_ref,
    own, other, shifted, kflux, kprev, rate, sent_state, sent_side, prev, codes,
    lines, side, line, fac, delta, back,
    load_sem, inst_sem, state_sem, side_sem, back_sem, self_sem, known,
):
    me = lax.axis_index("cell")
    inst = lax.axis_index("inst")
    depth = me >> 3

    barrier = pltpu.get_barrier_semaphore()
    for j in range(1, 4):
        pl.semaphore_signal(barrier, 1, device_id={"inst": inst ^ j})
    for j in range(1, 5):
        pl.semaphore_signal(barrier, 1, device_id={"cell": me ^ j})
    tell_depths(barrier, me, depth, 1)
    loads = [
        pltpu.make_async_copy(state_ref.at[:, :, :, c], own.at[:, :, c], load_sem.at[c])
        for c in range(2)
    ] + [
        pltpu.make_async_copy(rate_ref.at[:, c], rate.at[c], load_sem.at[2 + c]) for c in range(2)
    ]
    for copy in loads:
        copy.start()
    pl.semaphore_wait(barrier, 7 + depth_peers(depth, 1))
    pl.semaphore_signal(known.at[0], 1, device_id={"cell": me ^ 4})
    for copy in loads:
        copy.wait()

    to_pair = [
        pltpu.make_async_remote_copy(
            own.at[i],
            other.at[1, i],
            inst_sem.at[0, i],
            inst_sem.at[1, i],
            device_id={"inst": inst ^ 2},
        )
        for i in range(2)
    ]
    to_twin = pltpu.make_async_remote_copy(
        own, other.at[0], inst_sem.at[2, 0], inst_sem.at[2, 1], device_id={"inst": inst ^ 1}
    )
    to_forward = [
        pltpu.make_async_remote_copy(
            other.at[1, i],
            other.at[2, i],
            inst_sem.at[3, i],
            inst_sem.at[4, i],
            device_id={"inst": inst ^ 1},
        )
        for i in range(2)
    ]
    for copy in to_pair:
        copy.start()
    to_twin.start()

    invert_lines(next_ref, prev)
    pl.semaphore_wait(known.at[0], 1)
    tell_depths(known.at[1], me, depth, 1)
    rate_rows = pack(rate[0], rate[1])

    def pack_state(i, carry):
        for v in range(6):
            rows = pack(own[i, v, 0], own[i, v, 1])
            for half in range(2):
                sent_state[i, half, v] = rows[half]
        for half in range(2):
            sent_state[i, half, 6] = rate_rows[half]
        return carry

    lax.fori_loop(0, 2, pack_state, 0)
    pl.semaphore_wait(known.at[1], depth_peers(depth, 1))
    tell_depths(known.at[2], me, depth, 2)
    gather_lines(own, shifted, next_ref)
    pl.semaphore_wait(known.at[2], depth_peers(depth, 2))
    pl.semaphore_signal(known.at[3], 1, device_id={"cell": me ^ 32})

    def pitch_flux(i, carry):
        for c in range(2):
            here = [own[i, v, c] for v in range(6)]
            there = [shifted[i, v, c] for v in range(6)]
            _, vel_h, p_h, sound_h = primitives(here)
            _, vel_t, p_t, sound_t = primitives(there)
            flux_h = flux(here, vel_h, p_h, 2)
            flux_t = flux(there, vel_t, p_t, 2)
            radius = 0.25 * (jnp.abs(vel_h) + sound_h + jnp.abs(vel_t) + sound_t)
            for v in range(6):
                kflux[i, v, c] = 0.5 * (flux_h[v] + flux_t[v]) - radius * (there[v] - here[v])
        return carry

    lax.fori_loop(0, 2, pitch_flux, 0)
    gather_lines(kflux, kprev, prev)
    pl.semaphore_wait(known.at[3], 1)

    my_row = (me & 7) * 8 + (me >> 3)
    my_inst, my_half, my_chunk = me >> 5, (me >> 4) & 1, me & 15

    def send_state(peer):
        pltpu.make_async_remote_copy(
            sent_state.at[peer >> 5, (peer >> 4) & 1, :, peer & 15],
            lines.at[:, my_row],
            state_sem.at[0],
            state_sem.at[1],
            device_id={"cell": peer},
        ).start()

    farthest_first(me, send_state)
    my_state = pltpu.make_async_copy(
        sent_state.at[my_inst, my_half, :, my_chunk], lines.at[:, my_row], self_sem.at[0]
    )
    my_state.start()

    weights = [
        [[time_weight(inst, n, slot, m) for m in range(2)] for slot in range(4)] for n in range(2)
    ]
    for i in range(2):
        to_pair[i].wait_recv()
        to_forward[i].start()
    to_twin.wait_recv()
    for copy in to_forward:
        copy.wait_recv()

    def add_time(v, carry):
        totals = [[None, None], [None, None]]
        for c in range(2):
            planes = [[own[m, v, c] for m in range(2)]] + [
                [other[slot, m, v, c] for m in range(2)] for slot in range(3)
            ]
            for n in range(2):
                total = kprev[n, v, c] - kflux[n, v, c]
                for slot in range(4):
                    for m in range(2):
                        if slot == 0 and m == n:
                            continue
                        total = total - weights[n][slot][m] * planes[slot][m]
                totals[n][c] = total
        for n in range(2):
            rows = pack(totals[n][0], totals[n][1])
            for half in range(2):
                sent_side[n, half, v] = rows[half]
        return carry

    lax.fori_loop(0, 6, add_time, 0)

    def send_side(peer):
        pltpu.make_async_remote_copy(
            sent_side.at[peer >> 5, (peer >> 4) & 1, :, peer & 15],
            side.at[:, my_row],
            side_sem.at[0],
            side_sem.at[1],
            device_id={"cell": peer},
        ).start()

    farthest_first(me, send_side)
    my_side = pltpu.make_async_copy(
        sent_side.at[my_inst, my_half, :, my_chunk], side.at[:, my_row], self_sem.at[1]
    )
    my_side.start()

    codes[...] = jnp.zeros((8, LANES), jnp.int32)
    codes[0:2, 0:64] = codes_ref[...]
    lane = lax.broadcasted_iota(jnp.int32, (8, LANES), 1)
    tile = my_chunk * 4 + my_half * 2 + ((lane & (HALF - 1)) >> 5)
    end_codes = [
        jnp.take_along_axis(jnp.broadcast_to(codes[e : e + 1, :], (8, LANES)), tile, axis=1)
        for e in range(2)
    ]
    many = lines.at[:, pl.ds(0, CELLS - 1)]
    pltpu.make_async_copy(many, many, state_sem.at[1]).wait()
    my_state.wait()
    radius = line_terms(lines, end_codes, line)
    factorise(radius, [lines[6, 8 * p : 8 * p + 8, :] for p in range(8)], fac)
    few = side.at[:, pl.ds(0, CELLS - 1)]
    pltpu.make_async_copy(few, few, side_sem.at[1]).wait()
    my_side.wait()
    substitute(fac, side, line, delta)

    def send_back(peer):
        pltpu.make_async_remote_copy(
            delta.at[:, (peer & 7) * 8 + (peer >> 3)],
            back.at[my_inst, my_half, :, my_chunk],
            back_sem.at[0],
            back_sem.at[1],
            device_id={"cell": peer},
        ).start()

    farthest_first(me, send_back)
    my_back = pltpu.make_async_copy(
        delta.at[:, my_row], back.at[my_inst, my_half, :, my_chunk], self_sem.at[2]
    )
    my_back.start()
    for copy in (*to_pair, to_twin, *to_forward):
        copy.wait_send()
    pltpu.make_async_copy(many, many, state_sem.at[0]).wait()
    pltpu.make_async_copy(few, few, side_sem.at[0]).wait()
    pltpu.make_async_copy(few, few, back_sem.at[0]).wait()
    pltpu.make_async_copy(few, few, back_sem.at[1]).wait()
    my_back.wait()

    def finish(i, carry):
        for v in range(6):
            update = pack(back[i, 0, v], back[i, 1, v])
            for c in range(2):
                out_ref[pl.ds((i * 6 + v) * 2 * CHUNKS + c, CHUNKS, stride=2), :] = (
                    own[i, v, c] + update[c]
                )
        return carry

    lax.fori_loop(0, 2, finish, 0)


def local(state, pseudo_rate, line_next, face_codes):
    view = state.reshape(2, 6, 2, CHUNKS, LANES).transpose(0, 1, 3, 2, 4)
    rate = pseudo_rate.reshape(2, CHUNKS, LANES).transpose(1, 0, 2)
    block = (2, 6, 2, CHUNKS, LANES)
    in_vmem = pl.BlockSpec(memory_space=pltpu.VMEM)
    in_place = pl.BlockSpec(memory_space=pl.ANY)
    dma = pltpu.SemaphoreType.DMA
    rows = pl.pallas_call(
        kernel,
        out_shape=jax.ShapeDtypeStruct((2 * 6 * CHUNKS * 2, LANES), F32),
        in_specs=[in_place, in_place, in_vmem, in_vmem],
        out_specs=in_vmem,
        scratch_shapes=[
            pltpu.VMEM(block, F32),
            pltpu.VMEM((3,) + block, F32),
            pltpu.VMEM(block, F32),
            pltpu.VMEM(block, F32),
            pltpu.VMEM(block, F32),
            pltpu.VMEM((2, CHUNKS, LANES), F32),
            pltpu.VMEM((2, 2, 7, CHUNKS, LANES), F32),
            pltpu.VMEM((2, 2, 6, CHUNKS, LANES), F32),
            pltpu.VMEM((CHUNKS, LANES), jnp.int32),
            pltpu.VMEM((8, LANES), jnp.int32),
            pltpu.VMEM((7, CELLS, LANES), F32),
            pltpu.VMEM((6, CELLS, LANES), F32),
            pltpu.VMEM((6, CELLS, LANES), F32),
            pltpu.VMEM((FACTOR_PLANES, 8, LANES), F32),
            pltpu.VMEM((6, CELLS, LANES), F32),
            pltpu.VMEM((2, 2, 6, CHUNKS, LANES), F32),
            dma((4,)),
            dma((5, 2)),
            dma((2,)),
            dma((2,)),
            dma((2,)),
            dma((3,)),
            pltpu.SemaphoreType.REGULAR((4,)),
        ],
        compiler_params=pltpu.CompilerParams(collective_id=0, has_side_effects=True),
        name="line_implicit_step",
    )(view, rate, line_next.reshape(CHUNKS, LANES), face_codes)
    return rows.reshape(2, 6, CHUNKS, 2, LANES).transpose(0, 1, 3, 2, 4).reshape(state.shape)


def solution(mesh):
    placed = (P("inst", None, "cell", None), P("cell", None), P(), P())
    return jax.shard_map(
        local, mesh=mesh, in_specs=placed, out_specs=P("inst", None, "cell", None), check_vma=False
    )
```

```python
import jax
import jax.numpy as jnp
import numpy as np
from jax import lax
from jax.experimental import pallas as pl
from jax.experimental.pallas import tpu as pltpu
from jax.sharding import PartitionSpec as P

NT = 8
CELLS = 64
CHUNKS = 16
LANES = 128
HALF = 64
TILE_LINES = 32
GAMMA_GAS = 1.4
FREE_STATE = (1.0, 0.5, 0.0, 0.0, 2.625, 0.2)
F32 = jnp.float32
FACTOR_PLANES = 84


def spectral_table():
    offsets = np.arange(NT)[:, None] - np.arange(NT)[None, :]
    angles = np.pi * offsets / NT
    safe_sin = np.where(offsets == 0, 1.0, np.sin(angles))
    parity = np.where(np.mod(offsets, 2) == 0, -1.0, 1.0)
    return np.where(offsets == 0, 0.0, 0.5 * parity * np.cos(angles) / safe_sin)


def time_weight(inst, row, slot, column):
    table = spectral_table()
    values = [float(table[2 * i + row, 2 * (i ^ slot) + column]) for i in range(NT // 2)]
    weight = jnp.float32(values[3])
    for i in (2, 1, 0):
        weight = jnp.where(inst == i, jnp.float32(values[i]), weight)
    return weight


def primitives(cell):
    inverse = 1.0 / cell[0]
    vel_x = cell[1] * inverse
    vel_y = cell[2] * inverse
    vel_z = cell[3] * inverse
    pressure = 0.4 * (cell[4] - 0.5 * cell[0] * (vel_x * vel_x + vel_y * vel_y + vel_z * vel_z))
    sound = jnp.sqrt(GAMMA_GAS * pressure * inverse)
    return vel_x, vel_y, pressure, sound


def flux(cell, velocity, pressure, component):
    rows = [cell[v] * velocity for v in range(6)]
    rows[component] = rows[component] + pressure
    rows[4] = rows[4] + pressure * velocity
    return rows


def swap(x):
    return pltpu.roll(x, HALF, x.ndim - 1)


def low_lanes(shape):
    return lax.broadcasted_iota(jnp.int32, shape, len(shape) - 1) < HALF


def pack(cell_a, cell_b):
    low = low_lanes(cell_a.shape)
    return jnp.where(low, cell_a, swap(cell_b)), jnp.where(low, swap(cell_a), cell_b)


def following(planes, swapped, p):
    low = low_lanes((8, LANES))
    return jnp.where(low, swapped[p], swapped[min(p + 1, len(planes) - 1)])


def preceding(planes, swapped, p):
    low = low_lanes((8, LANES))
    return jnp.where(low, swapped[max(p - 1, 0)], swapped[p])


def line_terms(state_ref, codes, line_ref):
    low = low_lanes((8, LANES))
    plane = lax.broadcasted_iota(jnp.int32, (8, LANES), 0)
    cells = []
    for v in range(6):
        inner = [state_ref[v, 8 * p : 8 * p + 8, :] for p in range(8)]
        ends = []
        for block, code, keep_low in ((inner[0], codes[0], True), (inner[7], codes[1], False)):
            turned = swap(block)
            mirror = -turned if v == 1 else turned
            copied = jnp.where(low, block, turned) if keep_low else jnp.where(low, turned, block)
            inflow = jnp.full((8, LANES), FREE_STATE[v], F32)
            ends.append(jnp.where(code == 0, mirror, jnp.where(code == 1, inflow, copied)))
        before = jnp.where(plane == 0, ends[0], pltpu.roll(inner[7], 1, 0))
        after = jnp.where(plane == 7, ends[1], pltpu.roll(inner[0], 7, 0))
        cells.append([before] + inner + [after])
    parts = [primitives([cells[v][p] for v in range(6)]) for p in range(10)]
    speed = [q[0] for q in parts]
    pressure = [q[2] for q in parts]
    radius = [jnp.abs(q[0]) + q[3] for q in parts]
    turned = [swap(q) for q in pressure]
    sensor = []
    for p in range(10):
        up, down = following(pressure, turned, p), preceding(pressure, turned, p)
        sensor.append(
            jnp.abs(up - 2.0 * pressure[p] + down) / (up + 2.0 * pressure[p] + down)
        )
    turned_sensor = [swap(q) for q in sensor]
    turned_radius = [swap(q) for q in radius]
    second, fourth, face_radius = [], [], []
    for p in range(9):
        e2 = 0.25 * jnp.maximum(sensor[p], following(sensor, turned_sensor, p))
        second.append(e2)
        fourth.append(jnp.maximum(0.0, 0.03125 - e2))
        face_radius.append(0.5 * (radius[p] + following(radius, turned_radius, p)))
    for v in range(6):
        own = cells[v]
        turned = [swap(q) for q in own]
        moved = [own[p] * speed[p] for p in range(10)]
        if v == 1:
            moved = [moved[p] + pressure[p] for p in range(10)]
        if v == 4:
            moved = [moved[p] + pressure[p] * speed[p] for p in range(10)]
        turned_moved = [swap(q) for q in moved]
        faces = []
        for p in range(9):
            near = following(own, turned, p) - own[p]
            far = own[p + 1] - preceding(own, turned, p) - 3.0 * near
            faces.append(
                0.5 * (moved[p] + following(moved, turned_moved, p))
                - face_radius[p] * (second[p] * near - fourth[p] * far)
            )
        turned_faces = [swap(q) for q in faces]
        for p in range(8):
            line_ref[v, 8 * p : 8 * p + 8, :] = faces[p + 1] - preceding(
                faces, turned_faces, p + 1
            )
    return radius


def mat_mat(a, b):
    return a[0] * b[0] + a[1] * swap(b[1]), a[0] * b[1] + a[1] * swap(b[0])


def mat_vec(a, x):
    return a[0] * x + a[1] * swap(x)


def mat_inv(m):
    turned = swap(m[0])
    reciprocal = 1.0 / (m[0] * turned - m[1] * swap(m[1]))
    return turned * reciprocal, -m[1] * reciprocal


def plus(a, b):
    return tuple(x + y for x, y in zip(a, b))


def minus(a):
    return tuple(-x for x in a)


def rolled(members, shift):
    return tuple(pltpu.roll(m, shift % 8, m.ndim - 2) for m in members)


STEPS = (
    (0, 1, 2, False),
    (2, 3, 4, False),
    (4, 5, 6, False),
    (6, 7, 0, True),
    (1, 3, 5, False),
    (5, 7, 1, True),
    (3, 7, 3, True),
)
BEFORE = {
    0: (7, True),
    2: (1, False),
    4: (3, False),
    6: (5, False),
    1: (7, True),
    5: (3, False),
    3: (7, True),
}
AFTER = {0: 1, 2: 3, 4: 5, 6: 7, 1: 3, 5: 7, 3: 7}


def factorise(radius, rate, fac_ref):
    low = low_lanes((8, LANES))
    plane = lax.broadcasted_iota(jnp.int32, (8, LANES), 0)
    radius = (
        [jnp.where(plane == 0, 0.0, radius[0])]
        + radius[1:9]
        + [jnp.where(plane == 7, 0.0, radius[9])]
    )
    turned = [swap(q) for q in radius]
    sub, diag, sup = {}, {}, {}
    for p in range(8):
        b = radius[p + 1]
        a = preceding(radius, turned, p + 1)
        c = following(radius, turned, p + 1)
        lower, upper = -(a + b), -(b + c)
        middle = rate[p] * b + 0.5 * (a + 2.0 * b + c) + 0.25 * (a + 4.0 * b + c)
        sub[p] = (0.25 * a, jnp.where(low, lower, 0.0))
        diag[p] = (middle, jnp.where(low, upper, lower))
        sup[p] = (0.25 * c, jnp.where(low, 0.0, upper))
    sub[0] = tuple(jnp.where(plane == 0, 0.0, m) for m in sub[0])
    sup[7] = tuple(jnp.where(plane == 7, 0.0, m) for m in sup[7])
    count = [0]

    def keep(members):
        for m in members:
            fac_ref[count[0]] = m
            count[0] += 1

    inverse = {}
    for e, o, n, wraps in STEPS:
        for x in (e, n):
            if x not in inverse:
                inverse[x] = mat_inv(diag[x])
        inv_n, sub_n, sup_n = inverse[n], sub[n], sup[n]
        if wraps:
            inv_n, sub_n, sup_n = rolled(inv_n, -1), rolled(sub_n, -1), rolled(sup_n, -1)
        left = minus(mat_mat(sub[o], inverse[e]))
        right = minus(mat_mat(sup[o], inv_n))
        keep(left)
        keep(right)
        keep(inverse[e])
        keep(mat_mat(inverse[e], sub[e]))
        keep(mat_mat(inverse[e], sup[e]))
        sub[o] = mat_mat(left, sub[e])
        diag[o] = plus(diag[o], plus(mat_mat(left, sup[e]), mat_mat(right, sub_n)))
        sup[o] = mat_mat(right, sup_n)
    s, d, u = sub[7], diag[7], sup[7]
    for h in (1, 2, 4):
        inv = mat_inv(d)
        left = minus(mat_mat(s, rolled(inv, h)))
        right = minus(mat_mat(u, rolled(inv, -h)))
        keep(left)
        keep(right)
        s_low, u_low = rolled(s, h), rolled(u, h)
        s_high, u_high = rolled(s, -h), rolled(u, -h)
        d = plus(d, plus(mat_mat(left, u_low), mat_mat(right, s_high)))
        s, u = mat_mat(left, s_low), mat_mat(right, u_high)
    keep(mat_inv(d))


def substitute(fac_ref, side_ref, line_ref, out_ref):
    def fac(first):
        return fac_ref[first][None], fac_ref[first + 1][None]

    def shift(x, count):
        return pltpu.roll(x, count % 8, 1)

    r = [side_ref[:, 8 * p : 8 * p + 8, :] - line_ref[:, 8 * p : 8 * p + 8, :] for p in range(8)]
    at = 0
    bases = {}
    for e, o, n, wraps in STEPS:
        side_n = shift(r[n], -1) if wraps else r[n]
        r[o] = r[o] + (mat_vec(fac(at), r[e]) + mat_vec(fac(at + 2), side_n))
        bases[e] = at + 4
        at += 10
    x = r[7]
    for h in (1, 2, 4):
        x = x + (mat_vec(fac(at), shift(x, h)) + mat_vec(fac(at + 2), shift(x, -h)))
        at += 4
    values = {7: mat_vec(fac(at), x)}
    for e in (3, 5, 1, 6, 4, 2, 0):
        base = bases[e]
        prior, wraps = BEFORE[e]
        low = shift(values[prior], 1) if wraps else values[prior]
        back = mat_vec(fac(base + 2), low) + mat_vec(fac(base + 4), values[AFTER[e]])
        values[e] = mat_vec(fac(base), r[e]) - back
    for p in range(8):
        out_ref[:, 8 * p : 8 * p + 8, :] = values[p]


def invert_lines(next_ref, prev_ref):
    lane = lax.broadcasted_iota(jnp.int32, (CHUNKS, LANES), 1).astype(F32)
    chunk = lax.broadcasted_iota(jnp.int32, (CHUNKS, LANES), 0)
    slot = lax.broadcasted_iota(jnp.int32, (LANES, LANES), 0)
    total = jnp.zeros((CHUNKS, LANES), F32)
    for q in range(CHUNKS):
        row = next_ref[q : q + 1, :]
        hit = jnp.broadcast_to(row >> 7, (CHUNKS, LANES)) == chunk
        place = jnp.where(jnp.broadcast_to(row & 127, (LANES, LANES)) == slot, 1.0, 0.0)
        left = jnp.concatenate([jnp.where(hit, lane, 0.0), jnp.where(hit, 1.0, 0.0)], axis=0)
        found = lax.dot_general(
            left.astype(jnp.bfloat16),
            place.astype(jnp.bfloat16),
            (((1,), (1,)), ((), ())),
            preferred_element_type=F32,
        )
        total = total + (found[:CHUNKS] + found[CHUNKS:] * (q * 128.0))
    prev_ref[...] = total.astype(jnp.int32)


def gather_lines(source, target, index_ref):
    source_rows = source.reshape(24 * CHUNKS, LANES)
    target_rows = target.reshape(24 * CHUNKS, LANES)

    def body(c, carry):
        row = jnp.broadcast_to(index_ref[pl.ds(c, 1), :], (8, LANES))
        lane = row & 127
        chunk = row >> 7
        found = [jnp.zeros((8, LANES), F32) for _ in range(3)]
        for s in range(CHUNKS):
            hit = chunk == s
            for g in range(3):
                rows = source_rows[pl.ds(g * 8 * CHUNKS + s, 8, stride=CHUNKS), :]
                found[g] = jnp.where(hit, jnp.take_along_axis(rows, lane, axis=1), found[g])
        for g in range(3):
            target_rows[pl.ds(g * 8 * CHUNKS + c, 8, stride=CHUNKS), :] = found[g]
        return carry

    lax.fori_loop(0, CHUNKS, body, 0)


def farthest_first(me, send):
    for steps in ((4,), (3, 5), (2, 6), (1, 7), (0,)):
        planes = [((me >> 3) + step) & 7 for step in steps]

        def body(turn, carry, planes=planes):
            for plane in planes:
                send(plane, (me & 7) ^ (7 - turn))
            return carry

        lax.fori_loop(0, 8 if steps[0] else 7, body, 0)


def kernel(
    state_ref, rate_ref, next_ref, codes_ref, out_ref,
    own, other, shifted, kflux, kprev, rate, sent_state, sent_side, prev, codes,
    lines, side, line, fac, delta, back,
    load_sem, inst_sem, state_sem, side_sem, back_sem, self_sem, known,
):
    me = lax.axis_index("cell")
    inst = lax.axis_index("inst")
    depth = me >> 3

    barrier = pltpu.get_barrier_semaphore()
    for j in range(1, 4):
        pl.semaphore_signal(barrier, 1, device_id={"inst": inst ^ j})

    @pl.when(depth < 7)
    def _():
        pl.semaphore_signal(barrier, 1, device_id={"cell": 56 + (me & 7)})

    @pl.when(depth == 7)
    def _():
        for j in range(1, 5):
            pl.semaphore_signal(barrier, 1, device_id={"cell": me ^ j})

    loads = [
        pltpu.make_async_copy(state_ref.at[:, :, :, c], own.at[:, :, c], load_sem.at[c])
        for c in range(2)
    ] + [
        pltpu.make_async_copy(rate_ref.at[:, c], rate.at[c], load_sem.at[2 + c]) for c in range(2)
    ]
    for copy in loads:
        copy.start()
    pl.semaphore_wait(barrier, jnp.where(depth == 7, 14, 3))

    @pl.when(depth == 7)
    def _():
        for j in range(1, 4):
            pl.semaphore_signal(known.at[0], 1, device_id={"cell": me ^ j})

    for copy in loads:
        copy.wait()

    to_pair = [
        pltpu.make_async_remote_copy(
            own.at[i],
            other.at[1, i],
            inst_sem.at[0, i],
            inst_sem.at[1, i],
            device_id={"inst": inst ^ 2},
        )
        for i in range(2)
    ]
    to_twin = pltpu.make_async_remote_copy(
        own, other.at[0], inst_sem.at[2, 0], inst_sem.at[2, 1], device_id={"inst": inst ^ 1}
    )
    to_forward = [
        pltpu.make_async_remote_copy(
            other.at[1, i],
            other.at[2, i],
            inst_sem.at[3, i],
            inst_sem.at[4, i],
            device_id={"inst": inst ^ 1},
        )
        for i in range(2)
    ]
    for copy in to_pair:
        copy.start()
    to_twin.start()

    @pl.when(depth == 7)
    def _():
        pl.semaphore_wait(known.at[0], 3)
        pl.semaphore_signal(known.at[1], 1, device_id={"cell": me ^ 4})

    invert_lines(next_ref, prev)
    rate_rows = pack(rate[0], rate[1])

    def pack_state(i, carry):
        for v in range(6):
            rows = pack(own[i, v, 0], own[i, v, 1])
            for half in range(2):
                sent_state[i, half, v] = rows[half]
        for half in range(2):
            sent_state[i, half, 6] = rate_rows[half]
        return carry

    lax.fori_loop(0, 2, pack_state, 0)

    @pl.when(depth == 7)
    def _():
        pl.semaphore_wait(known.at[1], 1)
        for j in (4, 5, 3, 6, 2, 7, 1):
            pl.semaphore_signal(known.at[2], 1, device_id={"cell": me - 8 * j})

    gather_lines(own, shifted, next_ref)

    def pitch_flux(i, carry):
        for c in range(2):
            here = [own[i, v, c] for v in range(6)]
            there = [shifted[i, v, c] for v in range(6)]
            _, vel_h, p_h, sound_h = primitives(here)
            _, vel_t, p_t, sound_t = primitives(there)
            flux_h = flux(here, vel_h, p_h, 2)
            flux_t = flux(there, vel_t, p_t, 2)
            radius = 0.25 * (jnp.abs(vel_h) + sound_h + jnp.abs(vel_t) + sound_t)
            for v in range(6):
                kflux[i, v, c] = 0.5 * (flux_h[v] + flux_t[v]) - radius * (there[v] - here[v])
        return carry

    lax.fori_loop(0, 2, pitch_flux, 0)
    gather_lines(kflux, kprev, prev)
    for i in range(2):
        to_pair[i].wait_recv()
        to_forward[i].start()

    @pl.when(depth < 7)
    def _():
        pl.semaphore_wait(known.at[2], 1)


    my_row = (me & 7) * 8 + (me >> 3)
    my_inst, my_half, my_chunk = me >> 5, (me >> 4) & 1, me & 15

    def send_state(plane, place):
        pltpu.make_async_remote_copy(
            sent_state.at[plane >> 2, (plane >> 1) & 1, :, (plane & 1) * 8 + place],
            lines.at[:, my_row],
            state_sem.at[0],
            state_sem.at[1],
            device_id={"cell": plane * 8 + place},
        ).start()

    farthest_first(me, send_state)
    my_state = pltpu.make_async_copy(
        sent_state.at[my_inst, my_half, :, my_chunk], lines.at[:, my_row], self_sem.at[0]
    )
    my_state.start()

    weights = [
        [[time_weight(inst, n, slot, m) for m in range(2)] for slot in range(4)] for n in range(2)
    ]
    to_twin.wait_recv()
    for copy in to_forward:
        copy.wait_recv()

    def add_time(v, carry):
        totals = [[None, None], [None, None]]
        for c in range(2):
            planes = [[own[m, v, c] for m in range(2)]] + [
                [other[slot, m, v, c] for m in range(2)] for slot in range(3)
            ]
            for n in range(2):
                total = kprev[n, v, c] - kflux[n, v, c]
                for slot in range(4):
                    for m in range(2):
                        if slot == 0 and m == n:
                            continue
                        total = total - weights[n][slot][m] * planes[slot][m]
                totals[n][c] = total
        for n in range(2):
            rows = pack(totals[n][0], totals[n][1])
            for half in range(2):
                sent_side[n, half, v] = rows[half]
        return carry

    lax.fori_loop(0, 6, add_time, 0)

    def send_side(plane, place):
        pltpu.make_async_remote_copy(
            sent_side.at[plane >> 2, (plane >> 1) & 1, :, (plane & 1) * 8 + place],
            side.at[:, my_row],
            side_sem.at[0],
            side_sem.at[1],
            device_id={"cell": plane * 8 + place},
        ).start()

    farthest_first(me, send_side)
    my_side = pltpu.make_async_copy(
        sent_side.at[my_inst, my_half, :, my_chunk], side.at[:, my_row], self_sem.at[1]
    )
    my_side.start()

    codes[...] = jnp.zeros((8, LANES), jnp.int32)
    codes[0:2, 0:64] = codes_ref[...]
    lane = lax.broadcasted_iota(jnp.int32, (8, LANES), 1)
    tile = my_chunk * 4 + my_half * 2 + ((lane & (HALF - 1)) >> 5)
    end_codes = [
        jnp.take_along_axis(jnp.broadcast_to(codes[e : e + 1, :], (8, LANES)), tile, axis=1)
        for e in range(2)
    ]
    many = lines.at[:, pl.ds(0, CELLS - 1)]
    pltpu.make_async_copy(many, many, state_sem.at[1]).wait()
    my_state.wait()
    radius = line_terms(lines, end_codes, line)
    factorise(radius, [lines[6, 8 * p : 8 * p + 8, :] for p in range(8)], fac)
    few = side.at[:, pl.ds(0, CELLS - 1)]
    pltpu.make_async_copy(few, few, side_sem.at[1]).wait()
    my_side.wait()
    substitute(fac, side, line, delta)

    def send_back(plane, place):
        pltpu.make_async_remote_copy(
            delta.at[:, place * 8 + plane],
            back.at[my_inst, my_half, :, my_chunk],
            back_sem.at[0],
            back_sem.at[1],
            device_id={"cell": plane * 8 + place},
        ).start()

    farthest_first(me, send_back)
    my_back = pltpu.make_async_copy(
        delta.at[:, my_row], back.at[my_inst, my_half, :, my_chunk], self_sem.at[2]
    )
    my_back.start()
    for copy in (*to_pair, to_twin, *to_forward):
        copy.wait_send()
    pltpu.make_async_copy(many, many, state_sem.at[0]).wait()
    pltpu.make_async_copy(few, few, side_sem.at[0]).wait()
    pltpu.make_async_copy(few, few, back_sem.at[0]).wait()
    pltpu.make_async_copy(few, few, back_sem.at[1]).wait()
    my_back.wait()

    def finish(i, carry):
        for v in range(6):
            update = pack(back[i, 0, v], back[i, 1, v])
            for c in range(2):
                out_ref[pl.ds((i * 6 + v) * 2 * CHUNKS + c, CHUNKS, stride=2), :] = (
                    own[i, v, c] + update[c]
                )
        return carry

    lax.fori_loop(0, 2, finish, 0)


def local(state, pseudo_rate, line_next, face_codes):
    view = state.reshape(2, 6, 2, CHUNKS, LANES).transpose(0, 1, 3, 2, 4)
    rate = pseudo_rate.reshape(2, CHUNKS, LANES).transpose(1, 0, 2)
    block = (2, 6, 2, CHUNKS, LANES)
    in_vmem = pl.BlockSpec(memory_space=pltpu.VMEM)
    in_place = pl.BlockSpec(memory_space=pl.ANY)
    dma = pltpu.SemaphoreType.DMA
    rows = pl.pallas_call(
        kernel,
        out_shape=jax.ShapeDtypeStruct((2 * 6 * CHUNKS * 2, LANES), F32),
        in_specs=[in_place, in_place, in_vmem, in_vmem],
        out_specs=in_vmem,
        scratch_shapes=[
            pltpu.VMEM(block, F32),
            pltpu.VMEM((3,) + block, F32),
            pltpu.VMEM(block, F32),
            pltpu.VMEM(block, F32),
            pltpu.VMEM(block, F32),
            pltpu.VMEM((2, CHUNKS, LANES), F32),
            pltpu.VMEM((2, 2, 7, CHUNKS, LANES), F32),
            pltpu.VMEM((2, 2, 6, CHUNKS, LANES), F32),
            pltpu.VMEM((CHUNKS, LANES), jnp.int32),
            pltpu.VMEM((8, LANES), jnp.int32),
            pltpu.VMEM((7, CELLS, LANES), F32),
            pltpu.VMEM((6, CELLS, LANES), F32),
            pltpu.VMEM((6, CELLS, LANES), F32),
            pltpu.VMEM((FACTOR_PLANES, 8, LANES), F32),
            pltpu.VMEM((6, CELLS, LANES), F32),
            pltpu.VMEM((2, 2, 6, CHUNKS, LANES), F32),
            dma((4,)),
            dma((5, 2)),
            dma((2,)),
            dma((2,)),
            dma((2,)),
            dma((3,)),
            pltpu.SemaphoreType.REGULAR((3,)),
        ],
        compiler_params=pltpu.CompilerParams(collective_id=0, has_side_effects=True),
        name="line_implicit_step",
    )(view, rate, line_next.reshape(CHUNKS, LANES), face_codes)
    return rows.reshape(2, 6, CHUNKS, 2, LANES).transpose(0, 1, 3, 2, 4).reshape(state.shape)


def solution(mesh):
    placed = (P("inst", None, "cell", None), P("cell", None), P(), P())
    return jax.shard_map(
        local, mesh=mesh, in_specs=placed, out_specs=P("inst", None, "cell", None), check_vma=False
    )
```

```python
import jax
import jax.numpy as jnp
import numpy as np
from jax import lax
from jax.experimental import pallas as pl
from jax.experimental.pallas import tpu as pltpu
from jax.sharding import PartitionSpec as P

NT = 8
CELLS = 64
CHUNKS = 16
LANES = 128
HALF = 64
TILE_LINES = 32
GAMMA_GAS = 1.4
FREE_STATE = (1.0, 0.5, 0.0, 0.0, 2.625, 0.2)
F32 = jnp.float32
FACTOR_PLANES = 84


def spectral_table():
    offsets = np.arange(NT)[:, None] - np.arange(NT)[None, :]
    angles = np.pi * offsets / NT
    safe_sin = np.where(offsets == 0, 1.0, np.sin(angles))
    parity = np.where(np.mod(offsets, 2) == 0, -1.0, 1.0)
    return np.where(offsets == 0, 0.0, 0.5 * parity * np.cos(angles) / safe_sin)


def time_weight(inst, row, slot, column):
    table = spectral_table()
    values = [float(table[2 * i + row, 2 * (i ^ slot) + column]) for i in range(NT // 2)]
    weight = jnp.float32(values[3])
    for i in (2, 1, 0):
        weight = jnp.where(inst == i, jnp.float32(values[i]), weight)
    return weight


def primitives(cell):
    inverse = 1.0 / cell[0]
    vel_x = cell[1] * inverse
    vel_y = cell[2] * inverse
    vel_z = cell[3] * inverse
    pressure = 0.4 * (cell[4] - 0.5 * cell[0] * (vel_x * vel_x + vel_y * vel_y + vel_z * vel_z))
    sound = jnp.sqrt(GAMMA_GAS * pressure * inverse)
    return vel_x, vel_y, pressure, sound


def flux(cell, velocity, pressure, component):
    rows = [cell[v] * velocity for v in range(6)]
    rows[component] = rows[component] + pressure
    rows[4] = rows[4] + pressure * velocity
    return rows


def swap(x):
    return pltpu.roll(x, HALF, x.ndim - 1)


def low_lanes(shape):
    return lax.broadcasted_iota(jnp.int32, shape, len(shape) - 1) < HALF


def pack(cell_a, cell_b):
    low = low_lanes(cell_a.shape)
    return jnp.where(low, cell_a, swap(cell_b)), jnp.where(low, swap(cell_a), cell_b)


def following(planes, swapped, p):
    low = low_lanes((8, LANES))
    return jnp.where(low, swapped[p], swapped[min(p + 1, len(planes) - 1)])


def preceding(planes, swapped, p):
    low = low_lanes((8, LANES))
    return jnp.where(low, swapped[max(p - 1, 0)], swapped[p])


def line_terms(state_ref, codes, line_ref):
    low = low_lanes((8, LANES))
    plane = lax.broadcasted_iota(jnp.int32, (8, LANES), 0)
    cells = []
    for v in range(6):
        inner = [state_ref[v, 8 * p : 8 * p + 8, :] for p in range(8)]
        ends = []
        for block, code, keep_low in ((inner[0], codes[0], True), (inner[7], codes[1], False)):
            turned = swap(block)
            mirror = -turned if v == 1 else turned
            copied = jnp.where(low, block, turned) if keep_low else jnp.where(low, turned, block)
            inflow = jnp.full((8, LANES), FREE_STATE[v], F32)
            ends.append(jnp.where(code == 0, mirror, jnp.where(code == 1, inflow, copied)))
        before = jnp.where(plane == 0, ends[0], pltpu.roll(inner[7], 1, 0))
        after = jnp.where(plane == 7, ends[1], pltpu.roll(inner[0], 7, 0))
        cells.append([before] + inner + [after])
    parts = [primitives([cells[v][p] for v in range(6)]) for p in range(10)]
    speed = [q[0] for q in parts]
    pressure = [q[2] for q in parts]
    radius = [jnp.abs(q[0]) + q[3] for q in parts]
    turned = [swap(q) for q in pressure]
    sensor = []
    for p in range(10):
        up, down = following(pressure, turned, p), preceding(pressure, turned, p)
        sensor.append(
            jnp.abs(up - 2.0 * pressure[p] + down) / (up + 2.0 * pressure[p] + down)
        )
    turned_sensor = [swap(q) for q in sensor]
    turned_radius = [swap(q) for q in radius]
    second, fourth, face_radius = [], [], []
    for p in range(9):
        e2 = 0.25 * jnp.maximum(sensor[p], following(sensor, turned_sensor, p))
        second.append(e2)
        fourth.append(jnp.maximum(0.0, 0.03125 - e2))
        face_radius.append(0.5 * (radius[p] + following(radius, turned_radius, p)))
    for v in range(6):
        own = cells[v]
        turned = [swap(q) for q in own]
        moved = [own[p] * speed[p] for p in range(10)]
        if v == 1:
            moved = [moved[p] + pressure[p] for p in range(10)]
        if v == 4:
            moved = [moved[p] + pressure[p] * speed[p] for p in range(10)]
        turned_moved = [swap(q) for q in moved]
        faces = []
        for p in range(9):
            near = following(own, turned, p) - own[p]
            far = own[p + 1] - preceding(own, turned, p) - 3.0 * near
            faces.append(
                0.5 * (moved[p] + following(moved, turned_moved, p))
                - face_radius[p] * (second[p] * near - fourth[p] * far)
            )
        turned_faces = [swap(q) for q in faces]
        for p in range(8):
            line_ref[v, 8 * p : 8 * p + 8, :] = faces[p + 1] - preceding(
                faces, turned_faces, p + 1
            )
    return radius


def mat_mat(a, b):
    return a[0] * b[0] + a[1] * swap(b[1]), a[0] * b[1] + a[1] * swap(b[0])


def mat_vec(a, x):
    return a[0] * x + a[1] * swap(x)


def mat_inv(m):
    turned = swap(m[0])
    reciprocal = 1.0 / (m[0] * turned - m[1] * swap(m[1]))
    return turned * reciprocal, -m[1] * reciprocal


def plus(a, b):
    return tuple(x + y for x, y in zip(a, b))


def minus(a):
    return tuple(-x for x in a)


def rolled(members, shift):
    return tuple(pltpu.roll(m, shift % 8, m.ndim - 2) for m in members)


STEPS = (
    (0, 1, 2, False),
    (2, 3, 4, False),
    (4, 5, 6, False),
    (6, 7, 0, True),
    (1, 3, 5, False),
    (5, 7, 1, True),
    (3, 7, 3, True),
)
BEFORE = {
    0: (7, True),
    2: (1, False),
    4: (3, False),
    6: (5, False),
    1: (7, True),
    5: (3, False),
    3: (7, True),
}
AFTER = {0: 1, 2: 3, 4: 5, 6: 7, 1: 3, 5: 7, 3: 7}


def factorise(radius, rate, fac_ref):
    low = low_lanes((8, LANES))
    plane = lax.broadcasted_iota(jnp.int32, (8, LANES), 0)
    radius = (
        [jnp.where(plane == 0, 0.0, radius[0])]
        + radius[1:9]
        + [jnp.where(plane == 7, 0.0, radius[9])]
    )
    turned = [swap(q) for q in radius]
    sub, diag, sup = {}, {}, {}
    for p in range(8):
        b = radius[p + 1]
        a = preceding(radius, turned, p + 1)
        c = following(radius, turned, p + 1)
        lower, upper = -(a + b), -(b + c)
        middle = rate[p] * b + 0.5 * (a + 2.0 * b + c) + 0.25 * (a + 4.0 * b + c)
        sub[p] = (0.25 * a, jnp.where(low, lower, 0.0))
        diag[p] = (middle, jnp.where(low, upper, lower))
        sup[p] = (0.25 * c, jnp.where(low, 0.0, upper))
    sub[0] = tuple(jnp.where(plane == 0, 0.0, m) for m in sub[0])
    sup[7] = tuple(jnp.where(plane == 7, 0.0, m) for m in sup[7])
    count = [0]

    def keep(members):
        for m in members:
            fac_ref[count[0]] = m
            count[0] += 1

    inverse = {}
    for e, o, n, wraps in STEPS:
        for x in (e, n):
            if x not in inverse:
                inverse[x] = mat_inv(diag[x])
        inv_n, sub_n, sup_n = inverse[n], sub[n], sup[n]
        if wraps:
            inv_n, sub_n, sup_n = rolled(inv_n, -1), rolled(sub_n, -1), rolled(sup_n, -1)
        left = minus(mat_mat(sub[o], inverse[e]))
        right = minus(mat_mat(sup[o], inv_n))
        keep(left)
        keep(right)
        keep(inverse[e])
        keep(mat_mat(inverse[e], sub[e]))
        keep(mat_mat(inverse[e], sup[e]))
        sub[o] = mat_mat(left, sub[e])
        diag[o] = plus(diag[o], plus(mat_mat(left, sup[e]), mat_mat(right, sub_n)))
        sup[o] = mat_mat(right, sup_n)
    s, d, u = sub[7], diag[7], sup[7]
    for h in (1, 2, 4):
        inv = mat_inv(d)
        left = minus(mat_mat(s, rolled(inv, h)))
        right = minus(mat_mat(u, rolled(inv, -h)))
        keep(left)
        keep(right)
        s_low, u_low = rolled(s, h), rolled(u, h)
        s_high, u_high = rolled(s, -h), rolled(u, -h)
        d = plus(d, plus(mat_mat(left, u_low), mat_mat(right, s_high)))
        s, u = mat_mat(left, s_low), mat_mat(right, u_high)
    keep(mat_inv(d))


def substitute(fac_ref, side_ref, line_ref, out_ref):
    def fac(first):
        return fac_ref[first][None], fac_ref[first + 1][None]

    def shift(x, count):
        return pltpu.roll(x, count % 8, 1)

    r = [side_ref[:, 8 * p : 8 * p + 8, :] - line_ref[:, 8 * p : 8 * p + 8, :] for p in range(8)]
    at = 0
    bases = {}
    for e, o, n, wraps in STEPS:
        side_n = shift(r[n], -1) if wraps else r[n]
        r[o] = r[o] + (mat_vec(fac(at), r[e]) + mat_vec(fac(at + 2), side_n))
        bases[e] = at + 4
        at += 10
    x = r[7]
    for h in (1, 2, 4):
        x = x + (mat_vec(fac(at), shift(x, h)) + mat_vec(fac(at + 2), shift(x, -h)))
        at += 4
    values = {7: mat_vec(fac(at), x)}
    for e in (3, 5, 1, 6, 4, 2, 0):
        base = bases[e]
        prior, wraps = BEFORE[e]
        low = shift(values[prior], 1) if wraps else values[prior]
        back = mat_vec(fac(base + 2), low) + mat_vec(fac(base + 4), values[AFTER[e]])
        values[e] = mat_vec(fac(base), r[e]) - back
    for p in range(8):
        out_ref[:, 8 * p : 8 * p + 8, :] = values[p]


def invert_lines(next_ref, prev_ref):
    lane = lax.broadcasted_iota(jnp.int32, (CHUNKS, LANES), 1).astype(F32)
    chunk = lax.broadcasted_iota(jnp.int32, (CHUNKS, LANES), 0)
    slot = lax.broadcasted_iota(jnp.int32, (LANES, LANES), 0)
    total = jnp.zeros((CHUNKS, LANES), F32)
    for q in range(CHUNKS):
        row = next_ref[q : q + 1, :]
        hit = jnp.broadcast_to(row >> 7, (CHUNKS, LANES)) == chunk
        place = jnp.where(jnp.broadcast_to(row & 127, (LANES, LANES)) == slot, 1.0, 0.0)
        left = jnp.concatenate([jnp.where(hit, lane, 0.0), jnp.where(hit, 1.0, 0.0)], axis=0)
        found = lax.dot_general(
            left.astype(jnp.bfloat16),
            place.astype(jnp.bfloat16),
            (((1,), (1,)), ((), ())),
            preferred_element_type=F32,
        )
        total = total + (found[:CHUNKS] + found[CHUNKS:] * (q * 128.0))
    prev_ref[...] = total.astype(jnp.int32)


def gather_lines(source, target, index_ref):
    source_rows = source.reshape(24 * CHUNKS, LANES)
    target_rows = target.reshape(24 * CHUNKS, LANES)

    def body(c, carry):
        row = jnp.broadcast_to(index_ref[pl.ds(c, 1), :], (8, LANES))
        lane = row & 127
        chunk = row >> 7
        found = [jnp.zeros((8, LANES), F32) for _ in range(3)]
        for s in range(CHUNKS):
            hit = chunk == s
            for g in range(3):
                rows = source_rows[pl.ds(g * 8 * CHUNKS + s, 8, stride=CHUNKS), :]
                found[g] = jnp.where(hit, jnp.take_along_axis(rows, lane, axis=1), found[g])
        for g in range(3):
            target_rows[pl.ds(g * 8 * CHUNKS + c, 8, stride=CHUNKS), :] = found[g]
        return carry

    lax.fori_loop(0, CHUNKS, body, 0)


def farthest_first(me, send):
    for steps in ((4,), (3, 5), (2, 6), (1, 7), (0,)):
        planes = [((me >> 3) + step) & 7 for step in steps]

        def body(turn, carry, planes=planes):
            for plane in planes:
                send(plane, (me & 7) ^ (7 - turn))
            return carry

        lax.fori_loop(0, 8 if steps[0] else 7, body, 0)


def kernel(
    state_ref, rate_ref, next_ref, codes_ref, out_ref,
    own, other, shifted, kflux, kprev, rate, sent_state, sent_side, prev, codes,
    lines, side, line, fac, delta, back,
    load_sem, inst_sem, state_sem, side_sem, back_sem, self_sem, known,
):
    me = lax.axis_index("cell")
    inst = lax.axis_index("inst")
    depth = me >> 3

    barrier = pltpu.get_barrier_semaphore()
    for j in range(1, 4):
        pl.semaphore_signal(barrier, 1, device_id={"inst": inst ^ j})

    @pl.when(depth < 7)
    def _():
        pl.semaphore_signal(barrier, 1, device_id={"cell": 56 + (me & 7)})

    @pl.when(depth == 7)
    def _():
        for j in range(1, 5):
            pl.semaphore_signal(barrier, 1, device_id={"cell": me ^ j})

    loads = [
        pltpu.make_async_copy(state_ref.at[:, :, :, c], own.at[:, :, c], load_sem.at[c])
        for c in range(2)
    ] + [
        pltpu.make_async_copy(rate_ref.at[:, c], rate.at[c], load_sem.at[2 + c]) for c in range(2)
    ]
    for copy in loads:
        copy.start()
    pl.semaphore_wait(barrier, jnp.where(depth == 7, 14, 3))

    @pl.when(depth == 7)
    def _():
        for j in range(1, 4):
            pl.semaphore_signal(known.at[0], 1, device_id={"cell": me ^ j})

    for copy in loads:
        copy.wait()

    to_pair = [
        pltpu.make_async_remote_copy(
            own.at[i],
            other.at[1, i],
            inst_sem.at[0, i],
            inst_sem.at[1, i],
            device_id={"inst": inst ^ 2},
        )
        for i in range(2)
    ]
    to_twin = pltpu.make_async_remote_copy(
        own, other.at[0], inst_sem.at[2, 0], inst_sem.at[2, 1], device_id={"inst": inst ^ 1}
    )
    to_forward = [
        pltpu.make_async_remote_copy(
            other.at[1, i],
            other.at[2, i],
            inst_sem.at[3, i],
            inst_sem.at[4, i],
            device_id={"inst": inst ^ 1},
        )
        for i in range(2)
    ]
    for copy in to_pair:
        copy.start()
    to_twin.start()

    @pl.when(depth == 7)
    def _():
        pl.semaphore_wait(known.at[0], 3)
        pl.semaphore_signal(known.at[1], 1, device_id={"cell": me ^ 4})

    invert_lines(next_ref, prev)
    rate_rows = pack(rate[0], rate[1])

    def pack_state(i, carry):
        for v in range(6):
            rows = pack(own[i, v, 0], own[i, v, 1])
            for half in range(2):
                sent_state[i, half, v] = rows[half]
        for half in range(2):
            sent_state[i, half, 6] = rate_rows[half]
        return carry

    lax.fori_loop(0, 2, pack_state, 0)

    @pl.when(depth == 7)
    def _():
        pl.semaphore_wait(known.at[1], 1)
        for j in (4, 5, 3, 6, 2, 7, 1):
            pl.semaphore_signal(known.at[2], 1, device_id={"cell": me - 8 * j})

    my_row = (me & 7) * 8 + (me >> 3)
    my_inst, my_half, my_chunk = me >> 5, (me >> 4) & 1, me & 15

    def send_state(plane, place):
        pltpu.make_async_remote_copy(
            sent_state.at[plane >> 2, (plane >> 1) & 1, :, (plane & 1) * 8 + place],
            lines.at[:, my_row],
            state_sem.at[0],
            state_sem.at[1],
            device_id={"cell": plane * 8 + place},
        ).start()

    pl.when(depth == 7)(lambda: farthest_first(me, send_state))
    gather_lines(own, shifted, next_ref)

    def pitch_flux(i, carry):
        for c in range(2):
            here = [own[i, v, c] for v in range(6)]
            there = [shifted[i, v, c] for v in range(6)]
            _, vel_h, p_h, sound_h = primitives(here)
            _, vel_t, p_t, sound_t = primitives(there)
            flux_h = flux(here, vel_h, p_h, 2)
            flux_t = flux(there, vel_t, p_t, 2)
            radius = 0.25 * (jnp.abs(vel_h) + sound_h + jnp.abs(vel_t) + sound_t)
            for v in range(6):
                kflux[i, v, c] = 0.5 * (flux_h[v] + flux_t[v]) - radius * (there[v] - here[v])
        return carry

    lax.fori_loop(0, 2, pitch_flux, 0)
    gather_lines(kflux, kprev, prev)
    for i in range(2):
        to_pair[i].wait_recv()
        to_forward[i].start()

    @pl.when(depth < 7)
    def _():
        pl.semaphore_wait(known.at[2], 1)


    pl.when(depth < 7)(lambda: farthest_first(me, send_state))
    my_state = pltpu.make_async_copy(
        sent_state.at[my_inst, my_half, :, my_chunk], lines.at[:, my_row], self_sem.at[0]
    )
    my_state.start()

    weights = [
        [[time_weight(inst, n, slot, m) for m in range(2)] for slot in range(4)] for n in range(2)
    ]
    to_twin.wait_recv()
    for copy in to_forward:
        copy.wait_recv()

    def add_time(v, carry):
        totals = [[None, None], [None, None]]
        for c in range(2):
            planes = [[own[m, v, c] for m in range(2)]] + [
                [other[slot, m, v, c] for m in range(2)] for slot in range(3)
            ]
            for n in range(2):
                total = kprev[n, v, c] - kflux[n, v, c]
                for slot in range(4):
                    for m in range(2):
                        if slot == 0 and m == n:
                            continue
                        total = total - weights[n][slot][m] * planes[slot][m]
                totals[n][c] = total
        for n in range(2):
            rows = pack(totals[n][0], totals[n][1])
            for half in range(2):
                sent_side[n, half, v] = rows[half]
        return carry

    lax.fori_loop(0, 6, add_time, 0)

    def send_side(plane, place):
        pltpu.make_async_remote_copy(
            sent_side.at[plane >> 2, (plane >> 1) & 1, :, (plane & 1) * 8 + place],
            side.at[:, my_row],
            side_sem.at[0],
            side_sem.at[1],
            device_id={"cell": plane * 8 + place},
        ).start()

    farthest_first(me, send_side)
    my_side = pltpu.make_async_copy(
        sent_side.at[my_inst, my_half, :, my_chunk], side.at[:, my_row], self_sem.at[1]
    )
    my_side.start()

    codes[...] = jnp.zeros((8, LANES), jnp.int32)
    codes[0:2, 0:64] = codes_ref[...]
    lane = lax.broadcasted_iota(jnp.int32, (8, LANES), 1)
    tile = my_chunk * 4 + my_half * 2 + ((lane & (HALF - 1)) >> 5)
    end_codes = [
        jnp.take_along_axis(jnp.broadcast_to(codes[e : e + 1, :], (8, LANES)), tile, axis=1)
        for e in range(2)
    ]
    many = lines.at[:, pl.ds(0, CELLS - 1)]
    pltpu.make_async_copy(many, many, state_sem.at[1]).wait()
    my_state.wait()
    radius = line_terms(lines, end_codes, line)
    factorise(radius, [lines[6, 8 * p : 8 * p + 8, :] for p in range(8)], fac)
    few = side.at[:, pl.ds(0, CELLS - 1)]
    pltpu.make_async_copy(few, few, side_sem.at[1]).wait()
    my_side.wait()
    substitute(fac, side, line, delta)

    def send_back(plane, place):
        pltpu.make_async_remote_copy(
            delta.at[:, place * 8 + plane],
            back.at[my_inst, my_half, :, my_chunk],
            back_sem.at[0],
            back_sem.at[1],
            device_id={"cell": plane * 8 + place},
        ).start()

    farthest_first(me, send_back)
    my_back = pltpu.make_async_copy(
        delta.at[:, my_row], back.at[my_inst, my_half, :, my_chunk], self_sem.at[2]
    )
    my_back.start()
    for copy in (*to_pair, to_twin, *to_forward):
        copy.wait_send()
    pltpu.make_async_copy(many, many, state_sem.at[0]).wait()
    pltpu.make_async_copy(few, few, side_sem.at[0]).wait()
    pltpu.make_async_copy(few, few, back_sem.at[0]).wait()
    pltpu.make_async_copy(few, few, back_sem.at[1]).wait()
    my_back.wait()

    def finish(i, carry):
        for v in range(6):
            update = pack(back[i, 0, v], back[i, 1, v])
            for c in range(2):
                out_ref[pl.ds((i * 6 + v) * 2 * CHUNKS + c, CHUNKS, stride=2), :] = (
                    own[i, v, c] + update[c]
                )
        return carry

    lax.fori_loop(0, 2, finish, 0)


def hand_over(rows_ref, out_ref):
    out_ref[...] = rows_ref[...]


def local(state, pseudo_rate, line_next, face_codes):
    view = state.reshape(2, 6, 2, CHUNKS, LANES).transpose(0, 1, 3, 2, 4)
    rate = pseudo_rate.reshape(2, CHUNKS, LANES).transpose(1, 0, 2)
    block = (2, 6, 2, CHUNKS, LANES)
    in_vmem = pl.BlockSpec(memory_space=pltpu.VMEM)
    in_place = pl.BlockSpec(memory_space=pl.ANY)
    dma = pltpu.SemaphoreType.DMA
    rows = pl.pallas_call(
        kernel,
        out_shape=jax.ShapeDtypeStruct((2 * 6 * CHUNKS * 2, LANES), F32),
        in_specs=[in_place, in_place, in_vmem, in_vmem],
        out_specs=in_vmem,
        scratch_shapes=[
            pltpu.VMEM(block, F32),
            pltpu.VMEM((3,) + block, F32),
            pltpu.VMEM(block, F32),
            pltpu.VMEM(block, F32),
            pltpu.VMEM(block, F32),
            pltpu.VMEM((2, CHUNKS, LANES), F32),
            pltpu.VMEM((2, 2, 7, CHUNKS, LANES), F32),
            pltpu.VMEM((2, 2, 6, CHUNKS, LANES), F32),
            pltpu.VMEM((CHUNKS, LANES), jnp.int32),
            pltpu.VMEM((8, LANES), jnp.int32),
            pltpu.VMEM((7, CELLS, LANES), F32),
            pltpu.VMEM((6, CELLS, LANES), F32),
            pltpu.VMEM((6, CELLS, LANES), F32),
            pltpu.VMEM((FACTOR_PLANES, 8, LANES), F32),
            pltpu.VMEM((6, CELLS, LANES), F32),
            pltpu.VMEM((2, 2, 6, CHUNKS, LANES), F32),
            dma((4,)),
            dma((5, 2)),
            dma((2,)),
            dma((2,)),
            dma((2,)),
            dma((3,)),
            pltpu.SemaphoreType.REGULAR((3,)),
        ],
        compiler_params=pltpu.CompilerParams(collective_id=0, has_side_effects=True),
        name="line_implicit_step",
    )(view, rate, line_next.reshape(CHUNKS, LANES), face_codes)
    rows = pl.pallas_call(
        hand_over,
        out_shape=jax.ShapeDtypeStruct(rows.shape, F32),
        in_specs=[in_vmem],
        out_specs=in_vmem,
        name="hand_over",
    )(rows)
    return rows.reshape(2, 6, CHUNKS, 2, LANES).transpose(0, 1, 3, 2, 4).reshape(state.shape)


def solution(mesh):
    placed = (P("inst", None, "cell", None), P("cell", None), P(), P())
    return jax.shard_map(
        local, mesh=mesh, in_specs=placed, out_specs=P("inst", None, "cell", None), check_vma=False
    )
```

```python
import jax
import jax.numpy as jnp
import numpy as np
from jax import lax
from jax.experimental import pallas as pl
from jax.experimental.pallas import tpu as pltpu
from jax.sharding import PartitionSpec as P

NT = 8
CELLS = 64
CHUNKS = 16
LANES = 128
HALF = 64
TILE_LINES = 32
GAMMA_GAS = 1.4
FREE_STATE = (1.0, 0.5, 0.0, 0.0, 2.625, 0.2)
F32 = jnp.float32
FACTOR_PLANES = 84


def spectral_table():
    offsets = np.arange(NT)[:, None] - np.arange(NT)[None, :]
    angles = np.pi * offsets / NT
    safe_sin = np.where(offsets == 0, 1.0, np.sin(angles))
    parity = np.where(np.mod(offsets, 2) == 0, -1.0, 1.0)
    return np.where(offsets == 0, 0.0, 0.5 * parity * np.cos(angles) / safe_sin)


def time_weight(inst, row, slot, column):
    table = spectral_table()
    values = [float(table[2 * i + row, 2 * (i ^ slot) + column]) for i in range(NT // 2)]
    weight = jnp.float32(values[3])
    for i in (2, 1, 0):
        weight = jnp.where(inst == i, jnp.float32(values[i]), weight)
    return weight


def primitives(cell):
    inverse = 1.0 / cell[0]
    vel_x = cell[1] * inverse
    vel_y = cell[2] * inverse
    vel_z = cell[3] * inverse
    pressure = 0.4 * (cell[4] - 0.5 * cell[0] * (vel_x * vel_x + vel_y * vel_y + vel_z * vel_z))
    sound = jnp.sqrt(GAMMA_GAS * pressure * inverse)
    return vel_x, vel_y, pressure, sound


def flux(cell, velocity, pressure, component):
    rows = [cell[v] * velocity for v in range(6)]
    rows[component] = rows[component] + pressure
    rows[4] = rows[4] + pressure * velocity
    return rows


def swap(x):
    return pltpu.roll(x, HALF, x.ndim - 1)


def low_lanes(shape):
    return lax.broadcasted_iota(jnp.int32, shape, len(shape) - 1) < HALF


def pack(cell_a, cell_b):
    low = low_lanes(cell_a.shape)
    return jnp.where(low, cell_a, swap(cell_b)), jnp.where(low, swap(cell_a), cell_b)


def following(planes, swapped, p):
    low = low_lanes((8, LANES))
    return jnp.where(low, swapped[p], swapped[min(p + 1, len(planes) - 1)])


def preceding(planes, swapped, p):
    low = low_lanes((8, LANES))
    return jnp.where(low, swapped[max(p - 1, 0)], swapped[p])


def line_terms(state_ref, codes, line_ref):
    low = low_lanes((8, LANES))
    plane = lax.broadcasted_iota(jnp.int32, (8, LANES), 0)
    cells = []
    for v in range(6):
        inner = [state_ref[v, 8 * p : 8 * p + 8, :] for p in range(8)]
        ends = []
        for block, code, keep_low in ((inner[0], codes[0], True), (inner[7], codes[1], False)):
            turned = swap(block)
            mirror = -turned if v == 1 else turned
            copied = jnp.where(low, block, turned) if keep_low else jnp.where(low, turned, block)
            inflow = jnp.full((8, LANES), FREE_STATE[v], F32)
            ends.append(jnp.where(code == 0, mirror, jnp.where(code == 1, inflow, copied)))
        before = jnp.where(plane == 0, ends[0], pltpu.roll(inner[7], 1, 0))
        after = jnp.where(plane == 7, ends[1], pltpu.roll(inner[0], 7, 0))
        cells.append([before] + inner + [after])
    parts = [primitives([cells[v][p] for v in range(6)]) for p in range(10)]
    speed = [q[0] for q in parts]
    pressure = [q[2] for q in parts]
    radius = [jnp.abs(q[0]) + q[3] for q in parts]
    turned = [swap(q) for q in pressure]
    sensor = []
    for p in range(10):
        up, down = following(pressure, turned, p), preceding(pressure, turned, p)
        sensor.append(
            jnp.abs(up - 2.0 * pressure[p] + down) / (up + 2.0 * pressure[p] + down)
        )
    turned_sensor = [swap(q) for q in sensor]
    turned_radius = [swap(q) for q in radius]
    second, fourth, face_radius = [], [], []
    for p in range(9):
        e2 = 0.25 * jnp.maximum(sensor[p], following(sensor, turned_sensor, p))
        second.append(e2)
        fourth.append(jnp.maximum(0.0, 0.03125 - e2))
        face_radius.append(0.5 * (radius[p] + following(radius, turned_radius, p)))
    for v in range(6):
        own = cells[v]
        turned = [swap(q) for q in own]
        moved = [own[p] * speed[p] for p in range(10)]
        if v == 1:
            moved = [moved[p] + pressure[p] for p in range(10)]
        if v == 4:
            moved = [moved[p] + pressure[p] * speed[p] for p in range(10)]
        turned_moved = [swap(q) for q in moved]
        faces = []
        for p in range(9):
            near = following(own, turned, p) - own[p]
            far = own[p + 1] - preceding(own, turned, p) - 3.0 * near
            faces.append(
                0.5 * (moved[p] + following(moved, turned_moved, p))
                - face_radius[p] * (second[p] * near - fourth[p] * far)
            )
        turned_faces = [swap(q) for q in faces]
        for p in range(8):
            line_ref[v, 8 * p : 8 * p + 8, :] = faces[p + 1] - preceding(
                faces, turned_faces, p + 1
            )
    return radius


def mat_mat(a, b):
    return a[0] * b[0] + a[1] * swap(b[1]), a[0] * b[1] + a[1] * swap(b[0])


def mat_vec(a, x):
    return a[0] * x + a[1] * swap(x)


def mat_inv(m):
    turned = swap(m[0])
    reciprocal = 1.0 / (m[0] * turned - m[1] * swap(m[1]))
    return turned * reciprocal, -m[1] * reciprocal


def plus(a, b):
    return tuple(x + y for x, y in zip(a, b))


def minus(a):
    return tuple(-x for x in a)


def rolled(members, shift):
    return tuple(pltpu.roll(m, shift % 8, m.ndim - 2) for m in members)


STEPS = (
    (0, 1, 2, False),
    (2, 3, 4, False),
    (4, 5, 6, False),
    (6, 7, 0, True),
    (1, 3, 5, False),
    (5, 7, 1, True),
    (3, 7, 3, True),
)
BEFORE = {
    0: (7, True),
    2: (1, False),
    4: (3, False),
    6: (5, False),
    1: (7, True),
    5: (3, False),
    3: (7, True),
}
AFTER = {0: 1, 2: 3, 4: 5, 6: 7, 1: 3, 5: 7, 3: 7}


def factorise(radius, rate, fac_ref):
    low = low_lanes((8, LANES))
    plane = lax.broadcasted_iota(jnp.int32, (8, LANES), 0)
    radius = (
        [jnp.where(plane == 0, 0.0, radius[0])]
        + radius[1:9]
        + [jnp.where(plane == 7, 0.0, radius[9])]
    )
    turned = [swap(q) for q in radius]
    sub, diag, sup = {}, {}, {}
    for p in range(8):
        b = radius[p + 1]
        a = preceding(radius, turned, p + 1)
        c = following(radius, turned, p + 1)
        lower, upper = -(a + b), -(b + c)
        middle = rate[p] * b + 0.5 * (a + 2.0 * b + c) + 0.25 * (a + 4.0 * b + c)
        sub[p] = (0.25 * a, jnp.where(low, lower, 0.0))
        diag[p] = (middle, jnp.where(low, upper, lower))
        sup[p] = (0.25 * c, jnp.where(low, 0.0, upper))
    sub[0] = tuple(jnp.where(plane == 0, 0.0, m) for m in sub[0])
    sup[7] = tuple(jnp.where(plane == 7, 0.0, m) for m in sup[7])
    count = [0]

    def keep(members):
        for m in members:
            fac_ref[count[0]] = m
            count[0] += 1

    inverse = {}
    for e, o, n, wraps in STEPS:
        for x in (e, n):
            if x not in inverse:
                inverse[x] = mat_inv(diag[x])
        inv_n, sub_n, sup_n = inverse[n], sub[n], sup[n]
        if wraps:
            inv_n, sub_n, sup_n = rolled(inv_n, -1), rolled(sub_n, -1), rolled(sup_n, -1)
        left = minus(mat_mat(sub[o], inverse[e]))
        right = minus(mat_mat(sup[o], inv_n))
        keep(left)
        keep(right)
        keep(inverse[e])
        keep(mat_mat(inverse[e], sub[e]))
        keep(mat_mat(inverse[e], sup[e]))
        sub[o] = mat_mat(left, sub[e])
        diag[o] = plus(diag[o], plus(mat_mat(left, sup[e]), mat_mat(right, sub_n)))
        sup[o] = mat_mat(right, sup_n)
    s, d, u = sub[7], diag[7], sup[7]
    for h in (1, 2, 4):
        inv = mat_inv(d)
        left = minus(mat_mat(s, rolled(inv, h)))
        right = minus(mat_mat(u, rolled(inv, -h)))
        keep(left)
        keep(right)
        s_low, u_low = rolled(s, h), rolled(u, h)
        s_high, u_high = rolled(s, -h), rolled(u, -h)
        d = plus(d, plus(mat_mat(left, u_low), mat_mat(right, s_high)))
        s, u = mat_mat(left, s_low), mat_mat(right, u_high)
    keep(mat_inv(d))


def substitute(fac_ref, side_ref, line_ref, out_ref):
    def fac(first):
        return fac_ref[first][None], fac_ref[first + 1][None]

    def shift(x, count):
        return pltpu.roll(x, count % 8, 1)

    r = [side_ref[:, 8 * p : 8 * p + 8, :] - line_ref[:, 8 * p : 8 * p + 8, :] for p in range(8)]
    at = 0
    bases = {}
    for e, o, n, wraps in STEPS:
        side_n = shift(r[n], -1) if wraps else r[n]
        r[o] = r[o] + (mat_vec(fac(at), r[e]) + mat_vec(fac(at + 2), side_n))
        bases[e] = at + 4
        at += 10
    x = r[7]
    for h in (1, 2, 4):
        x = x + (mat_vec(fac(at), shift(x, h)) + mat_vec(fac(at + 2), shift(x, -h)))
        at += 4
    values = {7: mat_vec(fac(at), x)}
    for e in (3, 5, 1, 6, 4, 2, 0):
        base = bases[e]
        prior, wraps = BEFORE[e]
        low = shift(values[prior], 1) if wraps else values[prior]
        back = mat_vec(fac(base + 2), low) + mat_vec(fac(base + 4), values[AFTER[e]])
        values[e] = mat_vec(fac(base), r[e]) - back
    for p in range(8):
        out_ref[:, 8 * p : 8 * p + 8, :] = values[p]


def invert_lines(next_ref, prev_ref):
    lane = lax.broadcasted_iota(jnp.int32, (CHUNKS, LANES), 1).astype(F32)
    chunk = lax.broadcasted_iota(jnp.int32, (CHUNKS, LANES), 0)
    slot = lax.broadcasted_iota(jnp.int32, (LANES, LANES), 0)
    total = jnp.zeros((CHUNKS, LANES), F32)
    for q in range(CHUNKS):
        row = next_ref[q : q + 1, :]
        hit = jnp.broadcast_to(row >> 7, (CHUNKS, LANES)) == chunk
        place = jnp.where(jnp.broadcast_to(row & 127, (LANES, LANES)) == slot, 1.0, 0.0)
        left = jnp.concatenate([jnp.where(hit, lane, 0.0), jnp.where(hit, 1.0, 0.0)], axis=0)
        found = lax.dot_general(
            left.astype(jnp.bfloat16),
            place.astype(jnp.bfloat16),
            (((1,), (1,)), ((), ())),
            preferred_element_type=F32,
        )
        total = total + (found[:CHUNKS] + found[CHUNKS:] * (q * 128.0))
    prev_ref[...] = total.astype(jnp.int32)


def gather_lines(source, target, index_ref, turned):
    source_rows = source.reshape(24 * CHUNKS, LANES)
    target_rows = target.reshape(24 * CHUNKS, LANES)
    for s in range(CHUNKS):
        turned[s] = source_rows[pl.ds(s, 24, stride=CHUNKS), :]

    def body(c, carry):
        row = jnp.broadcast_to(index_ref[pl.ds(c, 1), :], (8, LANES))
        lane = row & 127
        chunk = row >> 7
        found = [jnp.zeros((8, LANES), F32) for _ in range(3)]
        for s in range(CHUNKS):
            hit = chunk == s
            for g in range(3):
                rows = turned[s, 8 * g : 8 * g + 8, :]
                found[g] = jnp.where(hit, jnp.take_along_axis(rows, lane, axis=1), found[g])
        for g in range(3):
            target_rows[pl.ds(g * 8 * CHUNKS + c, 8, stride=CHUNKS), :] = found[g]
        return carry

    lax.fori_loop(0, CHUNKS, body, 0)


def farthest_first(me, send):
    for steps in ((4,), (3, 5), (2, 6), (1, 7), (0,)):
        planes = [((me >> 3) + step) & 7 for step in steps]

        def body(turn, carry, planes=planes):
            for plane in planes:
                send(plane, (me & 7) ^ (7 - turn))
            return carry

        lax.fori_loop(0, 8 if steps[0] else 7, body, 0)


def kernel(
    state_ref, rate_ref, next_ref, codes_ref, out_ref,
    own, other, turned, shifted, kflux, kprev, rate, sent_state, sent_side, prev, codes,
    lines, side, line, fac, delta, back,
    load_sem, inst_sem, state_sem, side_sem, back_sem, self_sem, known,
):
    me = lax.axis_index("cell")
    inst = lax.axis_index("inst")
    depth = me >> 3

    barrier = pltpu.get_barrier_semaphore()
    for j in range(1, 4):
        pl.semaphore_signal(barrier, 1, device_id={"inst": inst ^ j})

    @pl.when(depth < 7)
    def _():
        pl.semaphore_signal(barrier, 1, device_id={"cell": 56 + (me & 7)})

    @pl.when(depth == 7)
    def _():
        for j in range(1, 5):
            pl.semaphore_signal(barrier, 1, device_id={"cell": me ^ j})

    loads = [
        pltpu.make_async_copy(state_ref.at[:, :, :, c], own.at[:, :, c], load_sem.at[c])
        for c in range(2)
    ] + [
        pltpu.make_async_copy(rate_ref.at[:, c], rate.at[c], load_sem.at[2 + c]) for c in range(2)
    ]
    for copy in loads:
        copy.start()
    pl.semaphore_wait(barrier, jnp.where(depth == 7, 14, 3))

    @pl.when(depth == 7)
    def _():
        for j in range(1, 4):
            pl.semaphore_signal(known.at[0], 1, device_id={"cell": me ^ j})

    for copy in loads:
        copy.wait()

    to_pair = [
        pltpu.make_async_remote_copy(
            own.at[i],
            other.at[1, i],
            inst_sem.at[0, i],
            inst_sem.at[1, i],
            device_id={"inst": inst ^ 2},
        )
        for i in range(2)
    ]
    to_twin = pltpu.make_async_remote_copy(
        own, other.at[0], inst_sem.at[2, 0], inst_sem.at[2, 1], device_id={"inst": inst ^ 1}
    )
    to_forward = [
        pltpu.make_async_remote_copy(
            other.at[1, i],
            other.at[2, i],
            inst_sem.at[3, i],
            inst_sem.at[4, i],
            device_id={"inst": inst ^ 1},
        )
        for i in range(2)
    ]
    for copy in to_pair:
        copy.start()
    to_twin.start()

    @pl.when(depth == 7)
    def _():
        pl.semaphore_wait(known.at[0], 3)
        pl.semaphore_signal(known.at[1], 1, device_id={"cell": me ^ 4})

    invert_lines(next_ref, prev)
    rate_rows = pack(rate[0], rate[1])

    def pack_state(i, carry):
        for v in range(6):
            rows = pack(own[i, v, 0], own[i, v, 1])
            for half in range(2):
                sent_state[i, half, v] = rows[half]
        for half in range(2):
            sent_state[i, half, 6] = rate_rows[half]
        return carry

    lax.fori_loop(0, 2, pack_state, 0)

    @pl.when(depth == 7)
    def _():
        pl.semaphore_wait(known.at[1], 1)
        for j in (4, 5, 3, 6, 2, 7, 1):
            pl.semaphore_signal(known.at[2], 1, device_id={"cell": me - 8 * j})

    my_row = (me & 7) * 8 + (me >> 3)
    my_inst, my_half, my_chunk = me >> 5, (me >> 4) & 1, me & 15

    def send_state(plane, place):
        pltpu.make_async_remote_copy(
            sent_state.at[plane >> 2, (plane >> 1) & 1, :, (plane & 1) * 8 + place],
            lines.at[:, my_row],
            state_sem.at[0],
            state_sem.at[1],
            device_id={"cell": plane * 8 + place},
        ).start()

    pl.when(depth == 7)(lambda: farthest_first(me, send_state))
    gather_lines(own, shifted, next_ref, turned)

    def pitch_flux(i, carry):
        for c in range(2):
            here = [own[i, v, c] for v in range(6)]
            there = [shifted[i, v, c] for v in range(6)]
            _, vel_h, p_h, sound_h = primitives(here)
            _, vel_t, p_t, sound_t = primitives(there)
            flux_h = flux(here, vel_h, p_h, 2)
            flux_t = flux(there, vel_t, p_t, 2)
            radius = 0.25 * (jnp.abs(vel_h) + sound_h + jnp.abs(vel_t) + sound_t)
            for v in range(6):
                kflux[i, v, c] = 0.5 * (flux_h[v] + flux_t[v]) - radius * (there[v] - here[v])
        return carry

    lax.fori_loop(0, 2, pitch_flux, 0)
    gather_lines(kflux, kprev, prev, turned)
    for i in range(2):
        to_pair[i].wait_recv()
        to_forward[i].start()

    @pl.when(depth < 7)
    def _():
        pl.semaphore_wait(known.at[2], 1)


    pl.when(depth < 7)(lambda: farthest_first(me, send_state))
    my_state = pltpu.make_async_copy(
        sent_state.at[my_inst, my_half, :, my_chunk], lines.at[:, my_row], self_sem.at[0]
    )
    my_state.start()

    weights = [
        [[time_weight(inst, n, slot, m) for m in range(2)] for slot in range(4)] for n in range(2)
    ]
    to_twin.wait_recv()
    for copy in to_forward:
        copy.wait_recv()

    def add_time(v, carry):
        totals = [[None, None], [None, None]]
        for c in range(2):
            planes = [[own[m, v, c] for m in range(2)]] + [
                [other[slot, m, v, c] for m in range(2)] for slot in range(3)
            ]
            for n in range(2):
                total = kprev[n, v, c] - kflux[n, v, c]
                for slot in range(4):
                    for m in range(2):
                        if slot == 0 and m == n:
                            continue
                        total = total - weights[n][slot][m] * planes[slot][m]
                totals[n][c] = total
        for n in range(2):
            rows = pack(totals[n][0], totals[n][1])
            for half in range(2):
                sent_side[n, half, v] = rows[half]
        return carry

    lax.fori_loop(0, 6, add_time, 0)

    def send_side(plane, place):
        pltpu.make_async_remote_copy(
            sent_side.at[plane >> 2, (plane >> 1) & 1, :, (plane & 1) * 8 + place],
            side.at[:, my_row],
            side_sem.at[0],
            side_sem.at[1],
            device_id={"cell": plane * 8 + place},
        ).start()

    farthest_first(me, send_side)
    my_side = pltpu.make_async_copy(
        sent_side.at[my_inst, my_half, :, my_chunk], side.at[:, my_row], self_sem.at[1]
    )
    my_side.start()

    codes[...] = jnp.zeros((8, LANES), jnp.int32)
    codes[0:2, 0:64] = codes_ref[...]
    lane = lax.broadcasted_iota(jnp.int32, (8, LANES), 1)
    tile = my_chunk * 4 + my_half * 2 + ((lane & (HALF - 1)) >> 5)
    end_codes = [
        jnp.take_along_axis(jnp.broadcast_to(codes[e : e + 1, :], (8, LANES)), tile, axis=1)
        for e in range(2)
    ]
    many = lines.at[:, pl.ds(0, CELLS - 1)]
    pltpu.make_async_copy(many, many, state_sem.at[1]).wait()
    my_state.wait()
    radius = line_terms(lines, end_codes, line)
    factorise(radius, [lines[6, 8 * p : 8 * p + 8, :] for p in range(8)], fac)
    few = side.at[:, pl.ds(0, CELLS - 1)]
    pltpu.make_async_copy(few, few, side_sem.at[1]).wait()
    my_side.wait()
    substitute(fac, side, line, delta)

    def send_back(plane, place):
        pltpu.make_async_remote_copy(
            delta.at[:, place * 8 + plane],
            back.at[my_inst, my_half, :, my_chunk],
            back_sem.at[0],
            back_sem.at[1],
            device_id={"cell": plane * 8 + place},
        ).start()

    farthest_first(me, send_back)
    my_back = pltpu.make_async_copy(
        delta.at[:, my_row], back.at[my_inst, my_half, :, my_chunk], self_sem.at[2]
    )
    my_back.start()
    for copy in (*to_pair, to_twin, *to_forward):
        copy.wait_send()
    pltpu.make_async_copy(many, many, state_sem.at[0]).wait()
    pltpu.make_async_copy(few, few, side_sem.at[0]).wait()
    pltpu.make_async_copy(few, few, back_sem.at[0]).wait()
    pltpu.make_async_copy(few, few, back_sem.at[1]).wait()
    my_back.wait()

    def finish(i, carry):
        for v in range(6):
            update = pack(back[i, 0, v], back[i, 1, v])
            for c in range(2):
                out_ref[pl.ds((i * 6 + v) * 2 * CHUNKS + c, CHUNKS, stride=2), :] = (
                    own[i, v, c] + update[c]
                )
        return carry

    lax.fori_loop(0, 2, finish, 0)


def hand_over(rows_ref, out_ref):
    out_ref[...] = rows_ref[...]


def local(state, pseudo_rate, line_next, face_codes):
    view = state.reshape(2, 6, 2, CHUNKS, LANES).transpose(0, 1, 3, 2, 4)
    rate = pseudo_rate.reshape(2, CHUNKS, LANES).transpose(1, 0, 2)
    block = (2, 6, 2, CHUNKS, LANES)
    in_vmem = pl.BlockSpec(memory_space=pltpu.VMEM)
    in_place = pl.BlockSpec(memory_space=pl.ANY)
    dma = pltpu.SemaphoreType.DMA
    rows = pl.pallas_call(
        kernel,
        out_shape=jax.ShapeDtypeStruct((2 * 6 * CHUNKS * 2, LANES), F32),
        in_specs=[in_place, in_place, in_vmem, in_vmem],
        out_specs=in_vmem,
        scratch_shapes=[
            pltpu.VMEM(block, F32),
            pltpu.VMEM((3,) + block, F32),
            pltpu.VMEM((CHUNKS, 24, LANES), F32),
            pltpu.VMEM(block, F32),
            pltpu.VMEM(block, F32),
            pltpu.VMEM(block, F32),
            pltpu.VMEM((2, CHUNKS, LANES), F32),
            pltpu.VMEM((2, 2, 7, CHUNKS, LANES), F32),
            pltpu.VMEM((2, 2, 6, CHUNKS, LANES), F32),
            pltpu.VMEM((CHUNKS, LANES), jnp.int32),
            pltpu.VMEM((8, LANES), jnp.int32),
            pltpu.VMEM((7, CELLS, LANES), F32),
            pltpu.VMEM((6, CELLS, LANES), F32),
            pltpu.VMEM((6, CELLS, LANES), F32),
            pltpu.VMEM((FACTOR_PLANES, 8, LANES), F32),
            pltpu.VMEM((6, CELLS, LANES), F32),
            pltpu.VMEM((2, 2, 6, CHUNKS, LANES), F32),
            dma((4,)),
            dma((5, 2)),
            dma((2,)),
            dma((2,)),
            dma((2,)),
            dma((3,)),
            pltpu.SemaphoreType.REGULAR((3,)),
        ],
        compiler_params=pltpu.CompilerParams(collective_id=0, has_side_effects=True),
        name="line_implicit_step",
    )(view, rate, line_next.reshape(CHUNKS, LANES), face_codes)
    rows = pl.pallas_call(
        hand_over,
        out_shape=jax.ShapeDtypeStruct(rows.shape, F32),
        in_specs=[in_vmem],
        out_specs=in_vmem,
        name="hand_over",
    )(rows)
    return rows.reshape(2, 6, CHUNKS, 2, LANES).transpose(0, 1, 3, 2, 4).reshape(state.shape)


def solution(mesh):
    placed = (P("inst", None, "cell", None), P("cell", None), P(), P())
    return jax.shard_map(
        local, mesh=mesh, in_specs=placed, out_specs=P("inst", None, "cell", None), check_vma=False
    )
```
